256 devices in a mesh: gx: 4 (over y), gy: 16 (over z, core), gz: 4 (over x).
Axes of the slice: x: 4, y: 4, z: 8, core: 2. Of those that a mesh axis runs over, the one named last changes fastest.
Arguments:
- flux_jacobian_factor: bfloat16 [4, 64, 8, 320, 320], P('gx', 'gy', 'gz'), may hold values from -6 to 6
- mass_over_timestep: float32 [4, 64, 8, 320], P('gx', 'gy', 'gz'), may hold values from 0.5 to 2
- face_jacobian: float32 [4, 64, 8, 3, 80, 160], P('gx', 'gy', 'gz'), may hold values from -1 to 1
- face_flags: int32 [4, 64, 8, 6], P('gx', 'gy', 'gz'), may hold values from 0 to 1, as said below
- right_side: float32 [4, 64, 8, 320], P('gx', 'gy', 'gz'), may hold values from -36 to 36
Outputs:
- update: float32 [4, 64, 8, 320], P('gx', 'gy', 'gz')
The draws below stay inside these ranges and needn't reach their ends.
Inputs may be any that keep to these rules, and one draw needn't show every extreme that they name: face_flags[e, 2 d] and face_flags[e, 2 d + 1] mark the lower and upper face of element e along dimension d as a wall (1) or open (0); the upper flag of an element along a dimension equals the lower flag of the element after it along that dimension.
All inputs are finite; a program needn't handle non-finite values.
Results may differ from the reference program's by a relative error of at most 0.0003.
Values sent between devices are 32-bit elements; how exact they have to be, the bound alone decides.
No kernel may reach another device: no remote copies, remote signals or barrier semaphores. Data moves between devices by JAX's collectives and lax.ppermute only.
A program may use at most 128 MiB of HBM per device.

```python
import math
import jax
import jax.numpy as jnp
from jax import lax

VARS = 5
ORDER = 4
KRYLOV = 3
ELEMENT_UNKNOWNS = 320
FACE_UNKNOWNS = 80
ELEMENTS_ALONG_X = 4
ELEMENTS_ALONG_Y = 64
ELEMENTS_ALONG_Z = 8


def draw_right_side(key, part):
    noise_key, magnitude_key = jax.random.split(key)
    array_extent = (ELEMENTS_ALONG_X, ELEMENTS_ALONG_Y, ELEMENTS_ALONG_Z, ELEMENT_UNKNOWNS)
    ramp = 1.0 + 2.0 * jnp.arange(ELEMENTS_ALONG_Y, dtype=jnp.float32) / (ELEMENTS_ALONG_Y - 1)
    element_magnitude = jnp.exp(jax.random.uniform(magnitude_key, (ELEMENTS_ALONG_X, ELEMENTS_ALONG_Y, ELEMENTS_ALONG_Z, 1), jnp.float32) * jnp.log(10.0))
    values = jnp.clip(jax.random.normal(noise_key, array_extent, jnp.float32), -6.0, 6.0)
    return 0.2 * ramp[None, :, None, None] * element_magnitude * values


def draw_face_jacobian(key, part):
    random_keys = jax.random.split(key, 3)
    array_extent = (ELEMENTS_ALONG_X, ELEMENTS_ALONG_Y, ELEMENTS_ALONG_Z, 3, FACE_UNKNOWNS, 2 * FACE_UNKNOWNS)
    spread = 0.3 / jnp.sqrt(2.0 * FACE_UNKNOWNS)
    noise = jnp.clip(jax.random.normal(random_keys[0], array_extent, jnp.float32), -6.0, 6.0) * spread
    row_index = jnp.arange(FACE_UNKNOWNS)[:, None]
    col_index = jnp.arange(2 * FACE_UNKNOWNS)[None, :]
    left_diag = (col_index == row_index).astype(jnp.float32)
    right_diag = (col_index == row_index + FACE_UNKNOWNS).astype(jnp.float32)
    positive_side = jax.random.uniform(random_keys[1], (ELEMENTS_ALONG_X, ELEMENTS_ALONG_Y, ELEMENTS_ALONG_Z, 3, FACE_UNKNOWNS, 1), jnp.float32, 0.3, 0.8)
    negative_side = jax.random.uniform(random_keys[2], (ELEMENTS_ALONG_X, ELEMENTS_ALONG_Y, ELEMENTS_ALONG_Z, 3, FACE_UNKNOWNS, 1), jnp.float32, 0.3, 0.8)
    return noise + positive_side * left_diag - negative_side * right_diag


def draw_face_flags(key, part):
    random_keys = jax.random.split(key, 3)
    samples_along_x = jax.random.randint(random_keys[0], (ELEMENTS_ALONG_X + 1, ELEMENTS_ALONG_Y, ELEMENTS_ALONG_Z), 0, 4)
    samples_along_y = jax.random.randint(random_keys[1], (ELEMENTS_ALONG_X, ELEMENTS_ALONG_Y + 1, ELEMENTS_ALONG_Z), 0, 4)
    samples_along_z = jax.random.randint(random_keys[2], (ELEMENTS_ALONG_X, ELEMENTS_ALONG_Y, ELEMENTS_ALONG_Z + 1), 0, 4)
    walls_x = jnp.where(samples_along_x == 0, 1, 0).astype(jnp.int32)
    walls_y = jnp.where(samples_along_y == 0, 1, 0).astype(jnp.int32)
    walls_z = jnp.where(samples_along_z == 0, 1, 0).astype(jnp.int32)
    return jnp.stack([walls_x[:-1], walls_x[1:], walls_y[:, :-1], walls_y[:, 1:], walls_z[:, :, :-1], walls_z[:, :, 1:]], axis=-1)


def block_scale(rng, dims, cuts, least, high):
    def one(position, parts):
        heights = jax.random.uniform(jax.random.fold_in(jax.random.fold_in(rng, 6), position), (parts,), jnp.float32, least / len(cuts), high / len(cuts))
        return jnp.repeat(jnp.exp(heights), dims[position] // parts).reshape((-1,) + (1,) * (len(dims) - position - 1))

    gain = one(*cuts[0])
    for cut in cuts[1:]:
        gain = gain * one(*cut)
    return gain


def centred(rng, dims, deviation, limit, cuts=(), kind=jnp.bfloat16):
    drawn = deviation * jax.random.normal(rng, dims, jnp.float32)
    if cuts:
        drawn = drawn * block_scale(rng, dims, cuts, -0.22, 0.18)
    return jnp.clip(drawn, -limit, limit).astype(kind)


def setup_inputs(seed: int = 0) -> dict:
    key_list = jax.random.split(jax.random.key(seed), 6)
    flux_jacobian_factor = centred(key_list[0], (ELEMENTS_ALONG_X, ELEMENTS_ALONG_Y, ELEMENTS_ALONG_Z, ELEMENT_UNKNOWNS, ELEMENT_UNKNOWNS), 1.0, 6.0, ((0, 4), (1, 16), (2, 4)))
    mass_over_timestep = jnp.clip(jnp.exp(math.log(2.0) - 1.3862944 * jax.random.uniform(key_list[1], (ELEMENTS_ALONG_X, ELEMENTS_ALONG_Y, ELEMENTS_ALONG_Z, ELEMENT_UNKNOWNS), jnp.float32) ** block_scale(key_list[1], (ELEMENTS_ALONG_X, ELEMENTS_ALONG_Y, ELEMENTS_ALONG_Z, ELEMENT_UNKNOWNS), ((0, 4), (1, 16), (2, 4)), -0.2, 0.2)), 0.5, 2.0)
    face_jacobian = draw_face_jacobian(jax.random.fold_in(key_list[5], 71), 0)
    face_flags = draw_face_flags(jax.random.fold_in(key_list[5], 71), 0)
    right_side = draw_right_side(jax.random.fold_in(key_list[5], 71), 0)
    return {"flux_jacobian_factor": flux_jacobian_factor, "mass_over_timestep": mass_over_timestep, "face_jacobian": face_jacobian, "face_flags": face_flags, "right_side": right_side}


full_precision = lax.Precision.HIGHEST
wall_weight = 0.5

def take_face(field, d, index):
    lead = field.shape[:3]
    cube = field.reshape(lead + (VARS, ORDER, ORDER, ORDER))
    face = lax.index_in_dim(cube, index, axis=4 + d, keepdims=False)
    return face.reshape(lead + (FACE_UNKNOWNS,))

def put_face(values, d, index):
    lead = values.shape[:3]
    cube = jnp.zeros(lead + (VARS, ORDER, ORDER, ORDER), values.dtype)
    spot = (slice(None),) * (4 + d) + (index,)
    cube = cube.at[spot].set(values.reshape(lead + (VARS, ORDER, ORDER)))
    return cube.reshape(lead + (ELEMENT_UNKNOWNS,))

def face_flux(matrix, left_trace, right_trace):
    paired = jnp.concatenate([left_trace, right_trace], axis=-1)
    return jnp.einsum('abcfg,abcg->abcf', matrix, paired, precision=full_precision)

def couple_faces(field, d, w_dim, face_flags, below_trace, top_flux):
    count = field.shape[d]
    lower_trace = take_face(field, d, 0)
    upper_trace = take_face(field, d, ORDER - 1)
    lower_flux = face_flux(w_dim, below_trace, lower_trace)
    upper_flux = jnp.concatenate([lax.slice_in_dim(lower_flux, 1, count, axis=d), top_flux(lower_flux, upper_trace)], axis=d)
    lower_open = (1 - face_flags[..., 2 * d:2 * d + 1]).astype(jnp.float32)
    upper_open = (1 - face_flags[..., 2 * d + 1:2 * d + 2]).astype(jnp.float32)
    lower_part = -lower_open * lower_flux + (1.0 - lower_open) * wall_weight * lower_trace
    upper_part = upper_open * upper_flux + (1.0 - upper_open) * wall_weight * upper_trace
    return put_face(lower_part, d, 0) + put_face(upper_part, d, ORDER - 1)

def least_squares(columns, start_norm):
    count = len(columns)
    cosines = []
    sine_terms = []
    target_values = [start_norm] + [jnp.zeros((), jnp.float32) for i in range(count)]
    triangle = []
    for j in range(count):
        column = list(columns[j])
        for i in range(j):
            first_entry = column[i]
            second_entry = column[i + 1]
            column[i] = cosines[i] * first_entry + sine_terms[i] * second_entry
            column[i + 1] = -sine_terms[i] * first_entry + cosines[i] * second_entry
        radius = jnp.sqrt(column[j] * column[j] + column[j + 1] * column[j + 1])
        cosine = column[j] / radius
        sine_part = column[j + 1] / radius
        cosines.append(cosine)
        sine_terms.append(sine_part)
        column[j] = radius
        target_values[j + 1] = -sine_part * target_values[j]
        target_values[j] = cosine * target_values[j]
        triangle.append(column[:j + 1])
    weights = [None] * count
    for i in reversed(range(count)):
        running = target_values[i]
        for k in range(i + 1, count):
            running = running - triangle[k][i] * weights[k]
        weights[i] = running / triangle[i][i]
    return weights

def invert_slab(items):
    factor_slab, mass_slab = items
    widened = factor_slab.astype(jnp.float32)
    gram_part = jnp.einsum('bcki,bckj->bcij', widened, widened, precision=full_precision)
    identity = jnp.eye(ELEMENT_UNKNOWNS, dtype=jnp.float32)
    jacobian = gram_part / ELEMENT_UNKNOWNS + mass_slab[..., None] * identity
    factor_lower = jnp.linalg.cholesky(jacobian)
    lower_inverse = jax.scipy.linalg.solve_triangular(factor_lower, jnp.broadcast_to(identity, jacobian.shape), lower=True)
    return jnp.einsum('bcki,bckj->bcij', lower_inverse, lower_inverse, precision=full_precision)

def jacobian_slab(items):
    factor_slab, mass_slab, field_slab = items
    widened = factor_slab.astype(jnp.float32)
    inner = jnp.einsum('bcki,bci->bck', widened, field_slab, precision=full_precision)
    outer = jnp.einsum('bcki,bck->bci', widened, inner, precision=full_precision)
    return outer / ELEMENT_UNKNOWNS + mass_slab * field_slab

def operator_apply(field, flux_jacobian_factor, mass_over_timestep, face_jacobian, face_flags):
    mapped = lax.map(jacobian_slab, (flux_jacobian_factor, mass_over_timestep, field))
    for d in range(3):
        count = field.shape[d]
        upper_trace = take_face(field, d, ORDER - 1)
        empty = jnp.zeros_like(lax.slice_in_dim(upper_trace, 0, 1, axis=d))
        below_trace = jnp.concatenate([empty, lax.slice_in_dim(upper_trace, 0, count - 1, axis=d)], axis=d)

        def top_flux(lower_flux, upper_values):
            return jnp.zeros_like(lax.slice_in_dim(lower_flux, 0, 1, axis=d))
        mapped = mapped + couple_faces(field, d, face_jacobian[:, :, :, d], face_flags, below_trace, top_flux)
    return mapped

def precond_apply(precond, vector):
    return jnp.einsum('abcij,abcj->abci', precond, vector, precision=full_precision)

def reference(flux_jacobian_factor, mass_over_timestep, face_jacobian, face_flags, right_side):
    precond = lax.map(invert_slab, (flux_jacobian_factor, mass_over_timestep))
    start_norm = jnp.sqrt(jnp.sum(right_side * right_side))
    krylov_basis = [right_side / start_norm]
    columns = []
    for j in range(KRYLOV):
        direction = precond_apply(precond, krylov_basis[j])
        mapped = operator_apply(direction, flux_jacobian_factor, mass_over_timestep, face_jacobian, face_flags)
        project = [jnp.sum(vector * mapped) for vector in krylov_basis]
        for i in range(len(krylov_basis)):
            mapped = mapped - project[i] * krylov_basis[i]
        length = jnp.sqrt(jnp.sum(mapped * mapped))
        columns.append(project + [length])
        if j + 1 < KRYLOV:
            krylov_basis.append(mapped / length)
    weights = least_squares(columns, start_norm)
    combined = weights[0] * krylov_basis[0]
    for j in range(1, KRYLOV):
        combined = combined + weights[j] * krylov_basis[j]
    return precond_apply(precond, combined)
```

```python
import jax
import jax.numpy as jnp
import numpy as np
from jax import lax
from jax.experimental import pallas as pl
from jax.experimental.pallas import tpu as pltpu
from jax.sharding import PartitionSpec as P

VARS = 5
ORDER = 4
KRYLOV = 3
UNKNOWNS = 320
FACE = 80
HEAD = 128
TAIL = UNKNOWNS - HEAD
CELLS = 8
LANES = 128
CONDITION_LIMIT = 40.0
wall_weight = 0.5

f32 = jnp.float32
bf16 = jnp.bfloat16
AXES = ("gx", "gy", "gz")


def face_nodes():
    cube = np.arange(UNKNOWNS).reshape(VARS, ORDER, ORDER, ORDER)
    nodes = []
    for d in range(3):
        for index in (0, ORDER - 1):
            nodes.append(np.take(cube, index, axis=1 + d).reshape(-1))
    return nodes


def gather_matrix():
    table = np.zeros((UNKNOWNS, 3 * 384), np.float32)
    nodes = face_nodes()
    for d in range(3):
        for k in range(FACE):
            table[nodes[2 * d + 1][k], 384 * d + k] = 1.0
            table[nodes[2 * d][k], 384 * d + LANES + FACE + k] = 1.0
    return table


def scatter_matrix():
    table = np.zeros((UNKNOWNS, 6 * FACE), np.float32)
    for side, nodes in enumerate(face_nodes()):
        for k in range(FACE):
            table[nodes[k], FACE * side + k] = 1.0
    return table


def wall_table():
    table = np.zeros((6, UNKNOWNS), np.float32)
    for side, nodes in enumerate(face_nodes()):
        table[side, nodes] = 1.0
    return table


def dot(a, b):
    return jnp.dot(a, b, preferred_element_type=f32)


def dot_nt(a, b):
    return lax.dot_general(a, b, (((1,), (1,)), ((), ())), preferred_element_type=f32)


def halves(a):
    high = a.astype(bf16)
    return high, (a - high.astype(f32)).astype(bf16)


def thirds(a):
    high = a.astype(bf16)
    rest = a - high.astype(f32)
    middle = rest.astype(bf16)
    return high, middle, (rest - middle.astype(f32)).astype(bf16)


def dot_split(a, b, product=dot):
    return product(a[0], b[0]) + (product(a[0], b[1]) + product(a[1], b[0]))


def eye_mask(n):
    rows = lax.broadcasted_iota(jnp.int32, (n, n), 0)
    cols = lax.broadcasted_iota(jnp.int32, (n, n), 1)
    return rows == cols


def approximate_inverses(blocks, lows):
    n = blocks[0].shape[0]
    diagonal = eye_mask(n)
    identity = jnp.where(diagonal, 1.0, 0.0)
    parts = [halves(a) for a in blocks]
    squares = [dot(p[0], p[0]) for p in parts]
    starts, errors, ratios = [], [], []
    for a, square, low in zip(blocks, squares, lows):
        sums = jnp.sum(jnp.abs(square), axis=0, keepdims=True)
        high = 1.03 * jnp.sqrt(jnp.max(sums, axis=1, keepdims=True))
        high = jnp.maximum(high, 1.1 * low)
        ratios.append(high / low)
        half = 0.5 * (high - low)
        mid = 0.5 * (high + low)
        inverse_half = 1.0 / half
        t = -mid * inverse_half
        t2 = t * t
        c3 = 16.0 * t
        c2 = 16.0 * t2 - 20.0
        c1 = t * c2
        c0 = t2 * c2 + 5.0
        top = t * c0
        gain = -inverse_half / top
        shifted = inverse_half * a + t * identity
        second = (inverse_half * inverse_half) * square + (2.0 * t) * shifted - t2 * identity
        inner = c3 * shifted + 16.0 * second
        outer = c1 * shifted + c2 * second + c0 * identity
        starts.append((second.astype(bf16), inner.astype(bf16), outer, gain))
        errors.append(1.0 / (top * top))
    firsts = [gain * (outer + dot(second, inner)) for second, inner, outer, gain in starts]
    narrow = [x.astype(bf16) for x in firsts]
    defects = [2.0 * identity - dot(p[0], x) for p, x in zip(parts, narrow)]
    seconds = [
        (2.0 / (2.0 - error)) * dot(x, e.astype(bf16))
        for x, e, error in zip(narrow, defects, errors)
    ]
    wide = [halves(x) for x in seconds]
    rests = [identity - dot_split(p, x) for p, x in zip(parts, wide)]
    small = [r.astype(bf16) for r in rests]
    sums = [r + dot(s, s) for r, s in zip(rests, small)]
    inverses = [
        x + dot_split(w, halves(s)) for x, w, s in zip(seconds, wide, sums)
    ]
    return inverses, ratios


def traces_of(field, gather):
    high, middle, low = thirds(field)
    stacked = jnp.concatenate([high.astype(f32), middle.astype(f32), low.astype(f32)], axis=0)
    out = dot(stacked.astype(bf16), gather)
    return out[0:8] + (out[8:16] + out[16:24])


def store_traces(traces, refs):
    for d in range(3):
        refs[2 * d][...] = traces[:, 384 * d : 384 * d + LANES]
        refs[2 * d + 1][...] = traces[:, 384 * d + LANES : 384 * (d + 1)]


def apply_inverses(inverse_ref, columns):
    rows = []
    for e in range(CELLS):
        rows.append(jnp.sum(inverse_ref[e] * columns[:, e : e + 1], axis=0, keepdims=True))
    return jnp.concatenate(rows, axis=0)


def invert_kernel(
    factor_ref, mass_ref, flags_ref, columns_ref, gather_ref, wall_ref,
    inverse_ref, walls_ref, field_ref, *trace_refs
):
    lows = []
    heads, crosses, backs, tails = [], [], [], []
    for e in range(CELLS):
        factor = factor_ref[e]
        left = factor[:, :HEAD]
        right = factor[:, HEAD:]
        left_t = left.T
        right_t = right.T
        scale = 1.0 / UNKNOWNS
        mass = mass_ref[e : e + 1, :]
        lows.append(jnp.min(mass, axis=1, keepdims=True))
        heads.append(scale * dot(left_t, left) + jnp.where(eye_mask(HEAD), mass[:, :HEAD], 0.0))
        crosses.append(scale * dot(left_t, right))
        backs.append(scale * dot(right_t, left))
        tails.append(scale * dot(right_t, right) + jnp.where(eye_mask(TAIL), mass[:, HEAD:], 0.0))
    firsts, ratios = approximate_inverses(heads, lows)
    first_parts = [halves(x) for x in firsts]
    carried = [dot_split(p, halves(c)) for p, c in zip(first_parts, crosses)]
    carried_parts = [halves(c) for c in carried]
    schurs = [
        tail - dot_split(halves(back), c) for tail, back, c in zip(tails, backs, carried_parts)
    ]
    lasts, more = approximate_inverses(schurs, lows)
    last_parts = [halves(x) for x in lasts]
    for e in range(CELLS):
        corner = -dot_split(carried_parts[e], last_parts[e])
        inverse_ref[e, HEAD:, HEAD:] = lasts[e]
        inverse_ref[e, :HEAD, HEAD:] = corner
        inverse_ref[e, HEAD:, :HEAD] = -dot_split(last_parts[e], carried_parts[e], dot_nt)
        inverse_ref[e, :HEAD, :HEAD] = firsts[e] - dot_split(halves(corner), carried_parts[e], dot_nt)
    worst = ratios[0]
    for ratio in ratios[1:] + more:
        worst = jnp.maximum(worst, ratio)

    @pl.when(jnp.logical_not(jnp.max(worst) <= CONDITION_LIMIT))
    def _():
        diagonal = eye_mask(UNKNOWNS)
        lane = lax.broadcasted_iota(jnp.int32, (1, UNKNOWNS), 1)
        line = lax.broadcasted_iota(jnp.int32, (UNKNOWNS, 1), 0)

        def element(e, carry):
            factor = factor_ref[e]
            mass = mass_ref[pl.ds(e, 1), :]
            inverse_ref[e] = dot(factor.T, factor) / UNKNOWNS + jnp.where(diagonal, mass, 0.0)

            def sweep(k, inner):
                table = inverse_ref[e]
                row = inverse_ref[e, pl.ds(k, 1), :]
                column = jnp.sum(jnp.where(diagonal, row, 0.0), axis=1, keepdims=True)
                pivot = jnp.sum(jnp.where(lane == k, row, 0.0), axis=1, keepdims=True)
                scaled = row / pivot
                swept = table - column * scaled
                swept = jnp.where(line == k, scaled, swept)
                swept = jnp.where(lane == k, column / pivot, swept)
                swept = jnp.where((line == k) & (lane == k), -1.0 / pivot, swept)
                inverse_ref[e] = swept
                return inner

            lax.fori_loop(0, UNKNOWNS, sweep, 0)
            inverse_ref[e] = -inverse_ref[e]
            return carry

        lax.fori_loop(0, CELLS, element, 0)

    walls_ref[...] = wall_weight * dot(flags_ref[...].astype(f32).astype(bf16), wall_ref[...])
    field = apply_inverses(inverse_ref, columns_ref[...])
    field_ref[...] = field
    store_traces(traces_of(field, gather_ref[...]), trace_refs)


def coupled(
    field_ref, walls_ref, flags_ref, face_ref, tops, own, received, scatter_ref
):
    lane8 = lax.broadcasted_iota(jnp.int32, (FACE, CELLS), 1)
    pieces = []
    for d, axis in enumerate(AXES):
        here = lax.axis_index(axis)
        has_below = here > 0
        has_above = here < lax.axis_size(axis) - 1
        upper = own[2 * d][...]
        lower = own[2 * d + 1][...]
        below = jnp.where(has_below, received[2 * d][...], 0.0)
        above = received[2 * d + 1][...]
        step = (CELLS, 2, 1)[d]
        count = (1, 4, 2)[d]
        upper_wide = jnp.concatenate([upper, jnp.zeros_like(upper)], axis=1)
        below_wide = jnp.concatenate([below, jnp.zeros_like(below)], axis=1)
        low_part = jnp.zeros((FACE, CELLS), f32)
        high_part = jnp.zeros((FACE, CELLS), f32)
        for e in range(CELLS):
            spot = (e // step) % count
            if spot == 0:
                other = e + step * (count - 1)
                left = below_wide[other : other + 1]
            else:
                left = upper_wide[e - step : e - step + 1]
            pair = left + lower[e : e + 1]
            flux = jnp.sum(face_ref[e, d] * pair[:, : 2 * FACE], axis=1, keepdims=True)
            closed = flags_ref[e, 2 * d] != 0
            flux = jnp.where(closed, 0.0, flux)
            low_part = jnp.where(lane8 == e, -flux, low_part)
            if spot > 0:
                high_part = jnp.where(lane8 == e - step, flux, high_part)
            if spot == count - 1:
                first = e - step * (count - 1)
                pair = upper_wide[e : e + 1] + above[first : first + 1]
                slot = (e, e - 6, e // 2)[d]
                flux = jnp.sum(tops[d][slot] * pair[:, : 2 * FACE], axis=1, keepdims=True)
                closed = flags_ref[e, 2 * d + 1] != 0
                flux = jnp.where(jnp.logical_and(jnp.logical_not(closed), has_above), flux, 0.0)
                high_part = jnp.where(lane8 == e, flux, high_part)
        pieces += [low_part, high_part]
    flux_columns = jnp.concatenate(pieces, axis=0)
    scatter = scatter_ref[...]
    high, middle, low = thirds(flux_columns)
    columns = dot(scatter, high) + (dot(scatter, middle) + dot(scatter, low))
    return columns + (walls_ref[...] * field_ref[...]).T


def split_refs(refs):
    own, received, tops = refs[:6], refs[6:12], refs[12:15]
    return own, received, tops, refs[15:]


def step_kernel(flags_ref, inverse_ref, walls_ref, gather_ref, scatter_ref, field_ref, face_ref, *refs):
    own, received, tops, outs = split_refs(refs)
    columns = coupled(field_ref, walls_ref, flags_ref, face_ref, tops, own, received, scatter_ref)
    outs[0][...] = columns
    field = apply_inverses(inverse_ref, columns)
    outs[1][...] = field
    store_traces(traces_of(field, gather_ref[...]), outs[2:])


def dots_kernel(flags_ref, walls_ref, scatter_ref, field_ref, face_ref, first_ref, second_ref, third_ref, *refs):
    own, received, tops, outs = split_refs(refs)
    last = coupled(field_ref, walls_ref, flags_ref, face_ref, tops, own, received, scatter_ref)
    vectors = [first_ref[...], second_ref[...], third_ref[...], last]
    lane = lax.broadcasted_iota(jnp.int32, (8, LANES), 1)
    packed = jnp.zeros((8, LANES), f32)
    for i in range(4):
        for j in range(i, 4):
            value = jnp.sum(jnp.sum(vectors[i] * vectors[j], axis=0, keepdims=True), axis=1, keepdims=True)
            packed = jnp.where(lane == 4 * i + j, value, packed)
    outs[0][...] = packed


def least_squares(columns, start_norm):
    count = len(columns)
    cosines = []
    sine_terms = []
    target_values = [start_norm] + [jnp.zeros_like(start_norm) for i in range(count)]
    triangle = []
    for j in range(count):
        column = list(columns[j])
        for i in range(j):
            first_entry = column[i]
            second_entry = column[i + 1]
            column[i] = cosines[i] * first_entry + sine_terms[i] * second_entry
            column[i + 1] = -sine_terms[i] * first_entry + cosines[i] * second_entry
        radius = jnp.sqrt(column[j] * column[j] + column[j + 1] * column[j + 1])
        cosine = column[j] / radius
        sine_part = column[j + 1] / radius
        cosines.append(cosine)
        sine_terms.append(sine_part)
        column[j] = radius
        target_values[j + 1] = -sine_part * target_values[j]
        target_values[j] = cosine * target_values[j]
        triangle.append(column[: j + 1])
    weights = [None] * count
    for i in reversed(range(count)):
        running = target_values[i]
        for k in range(i + 1, count):
            running = running - triangle[k][i] * weights[k]
        weights[i] = running / triangle[i][i]
    return weights


def finish_kernel(partial_ref, first_ref, second_ref, third_ref, out_ref):
    totals = jnp.sum(partial_ref[...], axis=0, keepdims=True)
    lane = lax.broadcasted_iota(jnp.int32, (1, LANES), 1)

    def entry(i, j):
        return jnp.sum(jnp.where(lane == 4 * i + j, totals, 0.0), axis=1, keepdims=True)

    upper = [[None] * 4 for i in range(4)]
    for i in range(4):
        for j in range(i, 4):
            value = entry(i, j)
            for k in range(i):
                value = value - upper[k][i] * upper[k][j]
            upper[i][j] = jnp.sqrt(value) if i == j else value / upper[i][i]
    columns = []
    for j in range(KRYLOV):
        column = []
        for i in range(j + 2):
            value = upper[i][j + 1]
            if i <= j:
                value = value + upper[i][j]
            column.append(value)
        columns.append(column)
    weights = least_squares(columns, upper[0][0])
    out_ref[...] = (
        weights[0] * first_ref[...] + weights[1] * second_ref[...] + weights[2] * third_ref[...]
    )


def vmem(count):
    return [pl.BlockSpec(memory_space=pltpu.VMEM)] * count


SMEM_SPEC = pl.BlockSpec(memory_space=pltpu.SMEM)


def call(kernel, specs, shapes, name, megabytes, args):
    return pl.pallas_call(
        kernel,
        out_shape=[jax.ShapeDtypeStruct(shape, f32) for shape in shapes],
        in_specs=specs,
        out_specs=vmem(len(shapes)),
        name=name,
        compiler_params=pltpu.CompilerParams(vmem_limit_bytes=megabytes << 20),
    )(*args)


TRACE_SHAPES = [(CELLS, LANES), (CELLS, 2 * LANES)] * 3


def around(block, axis, distance):
    count = lax.axis_size(axis)
    return lax.ppermute(block, axis, [(i, (i + distance) % count) for i in range(count)])


def exchanged(own):
    received = []
    for d, axis in enumerate(AXES):
        received.append(around(own[2 * d], axis, 1))
        received.append(around(own[2 * d + 1], axis, -1))
    return received


def shards(flux_jacobian_factor, mass_over_timestep, face_jacobian, face_flags, right_side):
    gather = jnp.asarray(gather_matrix(), bf16)
    scatter = jnp.asarray(scatter_matrix(), bf16)
    wall = jnp.asarray(wall_table(), bf16)
    flags = face_flags.reshape(CELLS, 6)
    faces = face_jacobian.reshape(CELLS, 3, FACE, 2 * FACE)
    tops = [
        around(face_jacobian[0:1, :, :, 0].reshape(8, FACE, 2 * FACE), "gx", -1),
        around(face_jacobian[:, 0:1, :, 1].reshape(2, FACE, 2 * FACE), "gy", -1),
        around(face_jacobian[:, :, 0:1, 2].reshape(4, FACE, 2 * FACE), "gz", -1),
    ]
    residual = right_side.reshape(CELLS, UNKNOWNS)
    vectors = [residual.T]
    inverse, walls, field, *own = call(
        invert_kernel,
        vmem(6),
        [(CELLS, UNKNOWNS, UNKNOWNS), (CELLS, UNKNOWNS), (CELLS, UNKNOWNS)] + TRACE_SHAPES,
        "invert",
        48,
        (
            flux_jacobian_factor.reshape(CELLS, UNKNOWNS, UNKNOWNS),
            mass_over_timestep.reshape(CELLS, UNKNOWNS),
            flags,
            vectors[0],
            gather,
            wall,
        ),
    )
    fields = [field]
    for j in range(KRYLOV - 1):
        received = exchanged(own)
        columns, field, *own = call(
            step_kernel,
            [SMEM_SPEC] + vmem(21),
            [(UNKNOWNS, CELLS), (CELLS, UNKNOWNS)] + TRACE_SHAPES,
            "step",
            24,
            (flags, inverse, walls, gather, scatter, fields[j], faces, *own, *received, *tops),
        )
        vectors.append(columns)
        fields.append(field)
    received = exchanged(own)
    (packed,) = call(
        dots_kernel,
        [SMEM_SPEC] + vmem(22),
        [(8, LANES)],
        "dots",
        24,
        (flags, walls, scatter, fields[2], faces, *vectors, *own, *received, *tops),
    )
    devices = lax.axis_size("gx") * lax.axis_size("gy") * lax.axis_size("gz")
    spread = jnp.broadcast_to(packed[0:1], (devices, LANES))
    partial = lax.all_to_all(spread, AXES, 0, 0, tiled=True)
    (update,) = call(
        finish_kernel, vmem(4), [(CELLS, UNKNOWNS)], "finish", 24, (partial, *fields)
    )
    return update.reshape(right_side.shape)


def solution(mesh):
    in_specs = (
        P("gx", "gy", "gz", None, None),
        P("gx", "gy", "gz", None),
        P("gx", "gy", "gz", None, None, None),
        P("gx", "gy", "gz", None),
        P("gx", "gy", "gz", None),
    )
    out_specs = P("gx", "gy", "gz", None)
    return jax.shard_map(shards, mesh=mesh, in_specs=in_specs, out_specs=out_specs, check_vma=False)
```

```python
import jax
import jax.numpy as jnp
import numpy as np
from jax import lax
from jax.experimental import pallas as pl
from jax.experimental.pallas import tpu as pltpu
from jax.sharding import PartitionSpec as P

VARS = 5
ORDER = 4
KRYLOV = 3
UNKNOWNS = 320
FACE = 80
HEAD = 128
TAIL = UNKNOWNS - HEAD
CELLS = 8
LANES = 128
CONDITION_LIMIT = 26.0
wall_weight = 0.5
INVERT_MIB = 28
STEP_MIB = 16


f32 = jnp.float32
bf16 = jnp.bfloat16
AXES = ("gx", "gy", "gz")
COUNTS = (1, 4, 2)
STEPS = (CELLS, 2, 1)


def face_nodes():
    cube = np.arange(UNKNOWNS).reshape(VARS, ORDER, ORDER, ORDER)
    nodes = []
    for d in range(3):
        for index in (0, ORDER - 1):
            nodes.append(np.take(cube, index, axis=1 + d).reshape(-1))
    return nodes


def gather_matrix():
    table = np.zeros((UNKNOWNS, 6 * LANES), np.float32)
    for side, nodes in enumerate(face_nodes()):
        for k in range(FACE):
            table[nodes[k], LANES * side + k] = 1.0
    return table


def scatter_matrix():
    table = np.zeros((UNKNOWNS, 6 * FACE), np.float32)
    for side, nodes in enumerate(face_nodes()):
        for k in range(FACE):
            table[nodes[k], FACE * side + k] = 1.0
    return table


def side_table():
    return np.repeat(np.eye(6, dtype=np.float32), FACE, axis=0)


def wall_table():
    table = np.zeros((6, UNKNOWNS), np.float32)
    for side, nodes in enumerate(face_nodes()):
        table[side, nodes] = 1.0
    return table


def dot(a, b):
    return jnp.dot(a, b, preferred_element_type=f32)


def dot_nt(a, b):
    return lax.dot_general(a, b, (((1,), (1,)), ((), ())), preferred_element_type=f32)


def halves(a):
    high = a.astype(bf16)
    return high, (a - high.astype(f32)).astype(bf16)


def thirds(a):
    high = a.astype(bf16)
    rest = a - high.astype(f32)
    middle = rest.astype(bf16)
    return high, middle, (rest - middle.astype(f32)).astype(bf16)


def dot_split(a, b, product=dot):
    return product(a[0], b[0]) + (product(a[0], b[1]) + product(a[1], b[0]))


def eye_mask(n):
    rows = lax.broadcasted_iota(jnp.int32, (n, n), 0)
    cols = lax.broadcasted_iota(jnp.int32, (n, n), 1)
    return rows == cols


def approximate_inverses(blocks, lows):
    n = blocks[0].shape[0]
    diagonal = eye_mask(n)
    identity = jnp.where(diagonal, 1.0, 0.0)
    parts = [halves(a) for a in blocks]
    squares = [dot(p[0], p[0]) for p in parts]
    firsts, errors, ratios = [], [], []
    for a, square, low in zip(blocks, squares, lows):
        sums = jnp.sum(jnp.abs(square), axis=0, keepdims=True)
        high = 1.03 * jnp.sqrt(jnp.max(sums, axis=1, keepdims=True))
        high = jnp.maximum(high, 1.1 * low)
        ratios.append(high / low)
        half = 0.5 * (high - low)
        scale = 1.0 / half
        t = -0.5 * (high + low) * scale
        t2 = t * t
        c3 = 16.0 * t
        c2 = 16.0 * t2 - 20.0
        c1 = t * c2
        c0 = t2 * c2 + 5.0
        top = t * c0
        gain = -scale / top
        square_scale = scale * scale
        slope = 2.0 * t * scale
        inner_slope = c3 * scale + 16.0 * slope
        both = c3 * t + 16.0 * t2
        outer = square_scale * square + slope * a
        inner = (16.0 * gain * square_scale) * square + (gain * inner_slope) * a
        by_square = gain * square_scale * (16.0 * t2 + both + c2)
        by_a = gain * (t2 * inner_slope + both * slope + c1 * scale + c2 * slope)
        by_one = gain * (t2 * both + c1 * t + c2 * t2 + c0)
        base = by_square * square + by_a * a + by_one * identity
        firsts.append(base + dot(outer.astype(bf16), inner.astype(bf16)))
        errors.append(1.0 / (top * top))
    narrow = [x.astype(bf16) for x in firsts]
    defects = [2.0 * identity - dot(p[0], x) for p, x in zip(parts, narrow)]
    seconds = [
        (2.0 / (2.0 - error)) * dot(x, e.astype(bf16))
        for x, e, error in zip(narrow, defects, errors)
    ]
    wide = [halves(x) for x in seconds]
    rests = [identity - dot_split(p, x) for p, x in zip(parts, wide)]
    small = [r.astype(bf16) for r in rests]
    sums = [r + dot(s, s) for r, s in zip(rests, small)]
    inverses = [
        x + dot(w[0], s.astype(bf16)) for x, w, s in zip(seconds, wide, sums)
    ]
    return inverses, ratios


def traces_of(field, gather):
    high, middle, low = thirds(field)
    stacked = jnp.concatenate([high.astype(f32), middle.astype(f32), low.astype(f32)], axis=0)
    out = dot(stacked.astype(bf16), gather)
    return out[0:8] + (out[8:16] + out[16:24])


def store_traces(traces, refs):
    for side in range(6):
        refs[side][...] = traces[:, LANES * side : LANES * (side + 1)]


def apply_inverses(inverse_ref, columns):
    rows = []
    for e in range(CELLS):
        rows.append(jnp.sum(inverse_ref[e] * columns[:, e : e + 1], axis=0, keepdims=True))
    return jnp.concatenate(rows, axis=0)


def rows_of(ref):
    return jnp.concatenate([ref[y] for y in range(ref.shape[0])], axis=0)


def invert_kernel(
    factor_hbm, mass_hbm, flags_hbm, residual_hbm, gather_hbm, wall_hbm, sides_hbm,
    inverse_ref, walls_ref, opens_ref, columns_ref, field_ref, *refs
):
    trace_refs, small_refs, (factor_ref, gather_ref, sems) = refs[:6], refs[6:11], refs[11:]
    mass_ref, flags_ref, residual_ref, wall_ref, sides_ref = small_refs
    sources = (mass_hbm, flags_hbm, residual_hbm, wall_hbm, sides_hbm)
    small_loads = [
        pltpu.make_async_copy(source, target, sems.at[CELLS + 1 + k])
        for k, (source, target) in enumerate(zip(sources, small_refs))
    ]
    loads = [
        pltpu.make_async_copy(factor_hbm.at[e], factor_ref.at[e], sems.at[e]) for e in range(CELLS)
    ]
    loads.append(pltpu.make_async_copy(gather_hbm, gather_ref, sems.at[CELLS]))
    for load in small_loads + loads:
        load.start()
    for load in small_loads:
        load.wait()
    masses = rows_of(mass_ref)
    columns = rows_of(residual_ref).T
    columns_ref[...] = columns
    flags = rows_of(flags_ref).astype(f32).astype(bf16)
    walls_ref[...] = wall_weight * dot(flags, wall_ref[...])
    open_sides = 1.0 - dot_nt(sides_ref[...], flags)
    side_lane = lax.broadcasted_iota(jnp.int32, (FACE, CELLS), 1)
    for d, axis in enumerate(AXES):
        step, count = STEPS[d], COUNTS[d]
        has_above = lax.axis_index(axis) < lax.axis_size(axis) - 1
        at_top = (side_lane // step) % count == count - 1
        opens_ref[2 * d * FACE : (2 * d + 1) * FACE] = -open_sides[2 * d * FACE : (2 * d + 1) * FACE]
        opens_ref[(2 * d + 1) * FACE : (2 * d + 2) * FACE] = jnp.where(
            jnp.logical_and(at_top, jnp.logical_not(has_above)),
            0.0,
            open_sides[(2 * d + 1) * FACE : (2 * d + 2) * FACE],
        )
    lows = []
    heads, crosses, backs, tails = [], [], [], []
    for e in range(CELLS):
        loads[e].wait()
        factor = factor_ref[e]
        left = factor[:, :HEAD]
        right = factor[:, HEAD:]
        left_t = left.T
        right_t = right.T
        scale = 1.0 / UNKNOWNS
        mass = masses[e : e + 1, :]
        lows.append(jnp.min(mass, axis=1, keepdims=True))
        heads.append(scale * dot(left_t, left) + jnp.where(eye_mask(HEAD), mass[:, :HEAD], 0.0))
        crosses.append(scale * dot(left_t, right))
        backs.append(scale * dot(right_t, left))
        tails.append(scale * dot(right_t, right) + jnp.where(eye_mask(TAIL), mass[:, HEAD:], 0.0))
    firsts, ratios = approximate_inverses(heads, lows)
    first_parts = [halves(x) for x in firsts]
    carried = [dot_split(p, halves(c)) for p, c in zip(first_parts, crosses)]
    carried_parts = [halves(c) for c in carried]
    schurs = [
        tail - dot_split(halves(back), c) for tail, back, c in zip(tails, backs, carried_parts)
    ]
    lasts, more = approximate_inverses(schurs, lows)
    last_parts = [halves(x) for x in lasts]
    for e in range(CELLS):
        corner = -dot_split(carried_parts[e], last_parts[e])
        inverse_ref[e, HEAD:, HEAD:] = lasts[e]
        inverse_ref[e, :HEAD, HEAD:] = corner
        inverse_ref[e, HEAD:, :HEAD] = corner.T
        inverse_ref[e, :HEAD, :HEAD] = firsts[e] - dot_split(halves(corner), carried_parts[e], dot_nt)
    worst = ratios[0]
    for ratio in ratios[1:] + more:
        worst = jnp.maximum(worst, ratio)

    @pl.when(jnp.logical_not(jnp.max(worst) <= CONDITION_LIMIT))
    def _():
        diagonal = eye_mask(UNKNOWNS)
        lane = lax.broadcasted_iota(jnp.int32, (1, UNKNOWNS), 1)
        line = lax.broadcasted_iota(jnp.int32, (UNKNOWNS, 1), 0)

        def element(e, carry):
            factor = factor_ref[e]
            line8 = lax.broadcasted_iota(jnp.int32, (CELLS, 1), 0)
            mass = jnp.sum(jnp.where(line8 == e, masses, 0.0), axis=0, keepdims=True)
            inverse_ref[e] = dot(factor.T, factor) / UNKNOWNS + jnp.where(diagonal, mass, 0.0)

            def sweep(k, inner):
                table = inverse_ref[e]
                row = inverse_ref[e, pl.ds(k, 1), :]
                column = jnp.sum(jnp.where(diagonal, row, 0.0), axis=1, keepdims=True)
                pivot = jnp.sum(jnp.where(lane == k, row, 0.0), axis=1, keepdims=True)
                scaled = row / pivot
                swept = table - column * scaled
                swept = jnp.where(line == k, scaled, swept)
                swept = jnp.where(lane == k, column / pivot, swept)
                swept = jnp.where((line == k) & (lane == k), -1.0 / pivot, swept)
                inverse_ref[e] = swept
                return inner

            lax.fori_loop(0, UNKNOWNS, sweep, 0)
            inverse_ref[e] = -inverse_ref[e]
            return carry

        lax.fori_loop(0, CELLS, element, 0)

    field = apply_inverses(inverse_ref, columns)
    field_ref[...] = field
    loads[CELLS].wait()
    store_traces(traces_of(field, gather_ref[...]), trace_refs)


def widened(trace):
    return jnp.concatenate([trace, jnp.zeros_like(trace)], axis=1)


def coupled(
    field_ref, walls_ref, opens_ref, face_ref, tops, own, received, scatter_ref
):
    lane8 = lax.broadcasted_iota(jnp.int32, (FACE, CELLS), 1)
    pieces = []
    for d, axis in enumerate(AXES):
        here = lax.axis_index(axis)
        has_below = here > 0
        lower = pltpu.roll(widened(own[2 * d][...]), FACE, 1)
        upper = widened(own[2 * d + 1][...])
        below = widened(jnp.where(has_below, received[2 * d][...], 0.0))
        above = pltpu.roll(widened(received[2 * d + 1][...]), FACE, 1)
        step, count = STEPS[d], COUNTS[d]
        faces = CELLS // count
        rest = above[:, LANES:]
        rests = [rest] + [pltpu.roll(rest, 32 * k, 1) for k in range(1, min(faces, 4))]
        low_part = jnp.zeros((FACE, CELLS), f32)
        high_part = jnp.zeros((FACE, CELLS), f32)
        for e in range(CELLS):
            spot = (e // step) % count
            if spot == 0:
                other = e + step * (count - 1)
                left = below[other : other + 1]
            else:
                left = upper[e - step : e - step + 1]
            pair = left + lower[e : e + 1]
            flux = jnp.sum(face_ref[e, d] * pair[:, : 2 * FACE], axis=1, keepdims=True)
            low_part = jnp.where(lane8 == e, flux, low_part)
            if spot > 0:
                high_part = jnp.where(lane8 == e - step, flux, high_part)
            if spot == count - 1:
                first = e - step * (count - 1)
                slot = (e, e - 6, e // 2)[d]
                pair = upper[e : e + 1, :LANES] + above[first : first + 1, :LANES]
                tail = rests[slot % 4][first : first + 1]
                flux = jnp.sum(
                    tops[d][slot] * pair + tops[d][faces + slot // 4] * tail, axis=1, keepdims=True
                )
                high_part = jnp.where(lane8 == e, flux, high_part)
        pieces += [low_part, high_part]
    flux_columns = opens_ref[...] * jnp.concatenate(pieces, axis=0)
    scatter = scatter_ref[...]
    high, middle, low = thirds(flux_columns)
    columns = dot(scatter, high) + (dot(scatter, middle) + dot(scatter, low))
    return columns + (walls_ref[...] * field_ref[...]).T


def split_refs(refs):
    own, received, tops = refs[:6], refs[6:12], refs[12:15]
    return own, received, tops, refs[15:]


def step_kernel(inverse_ref, walls_ref, opens_ref, gather_ref, scatter_ref, field_ref, face_ref, *refs):
    own, received, tops, outs = split_refs(refs)
    columns = coupled(field_ref, walls_ref, opens_ref, face_ref, tops, own, received, scatter_ref)
    outs[0][...] = columns
    field = apply_inverses(inverse_ref, columns)
    outs[1][...] = field
    store_traces(traces_of(field, gather_ref[...]), outs[2:])


def dots_kernel(walls_ref, opens_ref, scatter_ref, field_ref, face_ref, first_ref, second_ref, third_ref, *refs):
    own, received, tops, outs = split_refs(refs)
    last = coupled(field_ref, walls_ref, opens_ref, face_ref, tops, own, received, scatter_ref)
    vectors = [first_ref[...], second_ref[...], third_ref[...], last]
    lane = lax.broadcasted_iota(jnp.int32, (8, LANES), 1)
    packed = jnp.zeros((8, LANES), f32)
    for i in range(4):
        for j in range(i, 4):
            value = jnp.sum(jnp.sum(vectors[i] * vectors[j], axis=0, keepdims=True), axis=1, keepdims=True)
            packed = jnp.where(lane == 4 * i + j, value, packed)
    outs[0][...] = packed


def least_squares(columns, start_norm):
    count = len(columns)
    cosines = []
    sine_terms = []
    target_values = [start_norm] + [jnp.zeros_like(start_norm) for i in range(count)]
    triangle = []
    for j in range(count):
        column = list(columns[j])
        for i in range(j):
            first_entry = column[i]
            second_entry = column[i + 1]
            column[i] = cosines[i] * first_entry + sine_terms[i] * second_entry
            column[i + 1] = -sine_terms[i] * first_entry + cosines[i] * second_entry
        radius = jnp.sqrt(column[j] * column[j] + column[j + 1] * column[j + 1])
        cosine = column[j] / radius
        sine_part = column[j + 1] / radius
        cosines.append(cosine)
        sine_terms.append(sine_part)
        column[j] = radius
        target_values[j + 1] = -sine_part * target_values[j]
        target_values[j] = cosine * target_values[j]
        triangle.append(column[: j + 1])
    weights = [None] * count
    for i in reversed(range(count)):
        running = target_values[i]
        for k in range(i + 1, count):
            running = running - triangle[k][i] * weights[k]
        weights[i] = running / triangle[i][i]
    return weights


def finish_kernel(partial_ref, first_ref, second_ref, third_ref, out_ref):
    totals = jnp.sum(partial_ref[...], axis=0, keepdims=True)
    lane = lax.broadcasted_iota(jnp.int32, (1, LANES), 1)

    def entry(i, j):
        return jnp.sum(jnp.where(lane == 4 * i + j, totals, 0.0), axis=1, keepdims=True)

    upper = [[None] * 4 for i in range(4)]
    for i in range(4):
        for j in range(i, 4):
            value = entry(i, j)
            for k in range(i):
                value = value - upper[k][i] * upper[k][j]
            upper[i][j] = jnp.sqrt(value) if i == j else value / upper[i][i]
    columns = []
    for j in range(KRYLOV):
        column = []
        for i in range(j + 2):
            value = upper[i][j + 1]
            if i <= j:
                value = value + upper[i][j]
            column.append(value)
        columns.append(column)
    weights = least_squares(columns, upper[0][0])
    update = weights[0] * first_ref[...] + weights[1] * second_ref[...] + weights[2] * third_ref[...]
    for y in range(COUNTS[1]):
        out_ref[y] = update[2 * y : 2 * y + 2]


def vmem(count):
    return [pl.BlockSpec(memory_space=pltpu.VMEM)] * count


TOPS = [(e, 0) for e in range(CELLS)] + [(0, 1), (1, 1)] + [(e, 2) for e in (0, 2, 4, 6)]


def slabs_kernel(face_hbm, *refs):
    outs, (slab_ref, sems) = refs[:3], refs[3:]
    loads = []
    for slot, (e, d) in enumerate(TOPS):
        loads.append(pltpu.make_async_copy(face_hbm.at[e, d], slab_ref.at[slot], sems.at[slot]))
        loads[-1].start()
    for load in loads:
        load.wait()
    for d, (start, count) in enumerate(((0, CELLS), (CELLS, 2), (CELLS + 2, 4))):
        out = outs[d]
        for slot in range(count):
            out[slot] = slab_ref[start + slot, :, :LANES]
        for first in range(0, count, 4):
            group = [
                slab_ref[start + slot, :, LANES:] for slot in range(first, min(first + 4, count))
            ]
            if len(group) < 4:
                group.append(jnp.zeros((FACE, LANES - 32 * len(group)), f32))
            out[count + first // 4] = jnp.concatenate(group, axis=1)


HBM_SPEC = pl.BlockSpec(memory_space=pltpu.HBM)


def call(kernel, specs, shapes, name, megabytes, args, scratch=()):
    args = [
        pltpu.with_memory_space_constraint(arg, pltpu.HBM) if spec is HBM_SPEC else arg
        for arg, spec in zip(args, specs)
    ]
    return pl.pallas_call(
        kernel,
        out_shape=[jax.ShapeDtypeStruct(shape, f32) for shape in shapes],
        in_specs=specs,
        out_specs=vmem(len(shapes)),
        scratch_shapes=scratch,
        name=name,
        compiler_params=pltpu.CompilerParams(vmem_limit_bytes=megabytes << 20),
    )(*args)


TRACE_SHAPES = [(CELLS, LANES)] * 6
INVERT_SHAPES = [
    (CELLS, UNKNOWNS, UNKNOWNS),
    (CELLS, UNKNOWNS),
    (6 * FACE, CELLS),
    (UNKNOWNS, CELLS),
    (CELLS, UNKNOWNS),
] + TRACE_SHAPES
INVERT_SCRATCH = [
    pltpu.VMEM((4, 2, UNKNOWNS), f32),
    pltpu.VMEM((4, 2, 6), jnp.int32),
    pltpu.VMEM((4, 2, UNKNOWNS), f32),
    pltpu.VMEM((6, UNKNOWNS), bf16),
    pltpu.VMEM((6 * FACE, 6), bf16),
    pltpu.VMEM((CELLS, UNKNOWNS, UNKNOWNS), bf16),
    pltpu.VMEM((UNKNOWNS, 6 * LANES), bf16),
    pltpu.SemaphoreType.DMA((CELLS + 6,)),
]
SLAB_SHAPES = [(10, FACE, LANES), (3, FACE, LANES), (5, FACE, LANES)]


def around(block, axis, distance):
    count = lax.axis_size(axis)
    return lax.ppermute(block, axis, [(i, (i + distance) % count) for i in range(count)])


def exchanged(own):
    received = []
    for d, axis in enumerate(AXES):
        received.append(around(own[2 * d + 1], axis, 1))
        received.append(around(own[2 * d], axis, -1))
    return received


def shards(flux_jacobian_factor, mass_over_timestep, face_jacobian, face_flags, right_side):
    gather = jnp.asarray(gather_matrix(), bf16)
    scatter = jnp.asarray(scatter_matrix(), bf16)
    wall = jnp.asarray(wall_table(), bf16)
    sides = jnp.asarray(side_table(), bf16)
    faces = face_jacobian.reshape(CELLS, 3, FACE, 2 * FACE)
    slabs = call(
        slabs_kernel,
        [HBM_SPEC],
        SLAB_SHAPES,
        "slabs",
        8,
        (faces,),
        [pltpu.VMEM((len(TOPS), FACE, 2 * FACE), f32), pltpu.SemaphoreType.DMA((len(TOPS),))],
    )
    tops = [around(slab, axis, -1) for slab, axis in zip(slabs, AXES)]
    inverse, walls, opens, columns, field, *own = call(
        invert_kernel,
        [HBM_SPEC] * 7,
        INVERT_SHAPES,
        "invert",
        INVERT_MIB,
        (
            flux_jacobian_factor.reshape(CELLS, UNKNOWNS, UNKNOWNS),
            mass_over_timestep.reshape(4, 2, UNKNOWNS),
            face_flags.reshape(4, 2, 6),
            right_side.reshape(4, 2, UNKNOWNS),
            gather,
            wall,
            sides,
        ),
        INVERT_SCRATCH,
    )
    vectors, fields = [columns], [field]
    for j in range(KRYLOV - 1):
        received = exchanged(own)
        columns, field, *own = call(
            step_kernel,
            vmem(22),
            [(UNKNOWNS, CELLS), (CELLS, UNKNOWNS)] + TRACE_SHAPES,
            "step",
            STEP_MIB,
            (inverse, walls, opens, gather, scatter, fields[j], faces, *own, *received, *tops),
        )
        vectors.append(columns)
        fields.append(field)
    received = exchanged(own)
    (packed,) = call(
        dots_kernel,
        vmem(23),
        [(8, LANES)],
        "dots",
        STEP_MIB,
        (walls, opens, scatter, fields[2], faces, *vectors, *own, *received, *tops),
    )
    devices = lax.axis_size("gx") * lax.axis_size("gy") * lax.axis_size("gz")
    spread = jnp.broadcast_to(packed[0:1], (devices, LANES))
    partial = lax.all_to_all(spread, AXES, 0, 0, tiled=True)
    (update,) = call(
        finish_kernel, vmem(4), [(4, 2, UNKNOWNS)], "finish", 8, (partial, *fields)
    )
    return update.reshape(right_side.shape)


def solution(mesh):
    in_specs = (
        P("gx", "gy", "gz", None, None),
        P("gx", "gy", "gz", None),
        P("gx", "gy", "gz", None, None, None),
        P("gx", "gy", "gz", None),
        P("gx", "gy", "gz", None),
    )
    out_specs = P("gx", "gy", "gz", None)
    return jax.shard_map(shards, mesh=mesh, in_specs=in_specs, out_specs=out_specs, check_vma=False)
```

```python
import jax
import jax.numpy as jnp
import numpy as np
from jax import lax
from jax.experimental import pallas as pl
from jax.experimental.pallas import tpu as pltpu
from jax.sharding import PartitionSpec as P

VARS = 5
ORDER = 4
KRYLOV = 3
UNKNOWNS = 320
FACE = 80
HEAD = 128
TAIL = UNKNOWNS - HEAD
CELLS = 8
LANES = 128
CONDITION_LIMIT = 26.0
wall_weight = 0.5
INVERT_MIB = 28
STEP_MIB = 16


f32 = jnp.float32
bf16 = jnp.bfloat16
AXES = ("gx", "gy", "gz")
COUNTS = (1, 4, 2)
STEPS = (CELLS, 2, 1)


def face_nodes():
    cube = np.arange(UNKNOWNS).reshape(VARS, ORDER, ORDER, ORDER)
    nodes = []
    for d in range(3):
        for index in (0, ORDER - 1):
            nodes.append(np.take(cube, index, axis=1 + d).reshape(-1))
    return nodes


def gather_matrix():
    table = np.zeros((UNKNOWNS, 6 * LANES), np.float32)
    for side, nodes in enumerate(face_nodes()):
        for k in range(FACE):
            table[nodes[k], LANES * side + k] = 1.0
    return table


def scatter_matrix():
    table = np.zeros((UNKNOWNS, 6 * FACE), np.float32)
    for side, nodes in enumerate(face_nodes()):
        for k in range(FACE):
            table[nodes[k], FACE * side + k] = 1.0
    return table


def side_table():
    return np.repeat(np.eye(6, dtype=np.float32), FACE, axis=0)


def wall_table():
    table = np.zeros((6, UNKNOWNS), np.float32)
    for side, nodes in enumerate(face_nodes()):
        table[side, nodes] = 1.0
    return table


def dot(a, b):
    return jnp.dot(a, b, preferred_element_type=f32)


def dot_nt(a, b):
    return lax.dot_general(a, b, (((1,), (1,)), ((), ())), preferred_element_type=f32)


def halves(a):
    high = a.astype(bf16)
    return high, (a - high.astype(f32)).astype(bf16)


def thirds(a):
    high = a.astype(bf16)
    rest = a - high.astype(f32)
    middle = rest.astype(bf16)
    return high, middle, (rest - middle.astype(f32)).astype(bf16)


def dot_both(a, b):
    rows = a[0].shape[0]
    both = dot(jnp.concatenate(a, axis=0), b)
    return both[:rows] + both[rows:]


def dot_split(a, b):
    return dot_both(a, b[0]) + dot(a[0], b[1])


def dot_split_nt(a, b):
    rows = a[0].shape[0]
    both = dot_nt(jnp.concatenate(a, axis=0), b[0])
    return both[:rows] + (both[rows:] + dot_nt(a[0], b[1]))


def eye_mask(n):
    rows = lax.broadcasted_iota(jnp.int32, (n, n), 0)
    cols = lax.broadcasted_iota(jnp.int32, (n, n), 1)
    return rows == cols


def approximate_inverses(blocks, lows):
    n = blocks[0].shape[0]
    diagonal = eye_mask(n)
    identity = jnp.where(diagonal, 1.0, 0.0)
    parts = [halves(a) for a in blocks]
    squares = [dot(p[0], p[0]) for p in parts]
    firsts, errors, ratios = [], [], []
    for a, square, low in zip(blocks, squares, lows):
        sums = jnp.sum(jnp.abs(square), axis=0, keepdims=True)
        high = 1.03 * jnp.sqrt(jnp.max(sums, axis=1, keepdims=True))
        high = jnp.maximum(high, 1.1 * low)
        ratios.append(high / low)
        half = 0.5 * (high - low)
        scale = 1.0 / half
        t = -0.5 * (high + low) * scale
        t2 = t * t
        c3 = 16.0 * t
        c2 = 16.0 * t2 - 20.0
        c1 = t * c2
        c0 = t2 * c2 + 5.0
        top = t * c0
        gain = -scale / top
        square_scale = scale * scale
        slope = 2.0 * t * scale
        inner_slope = c3 * scale + 16.0 * slope
        both = c3 * t + 16.0 * t2
        outer = square_scale * square + slope * a
        inner = (16.0 * gain * square_scale) * square + (gain * inner_slope) * a
        by_square = gain * square_scale * (16.0 * t2 + both + c2)
        by_a = gain * (t2 * inner_slope + both * slope + c1 * scale + c2 * slope)
        by_one = gain * (t2 * both + c1 * t + c2 * t2 + c0)
        base = by_square * square + by_a * a + by_one * identity
        firsts.append(base + dot(outer.astype(bf16), inner.astype(bf16)))
        errors.append(1.0 / (top * top))
    narrow = [x.astype(bf16) for x in firsts]
    defects = [2.0 * identity - dot(p[0], x) for p, x in zip(parts, narrow)]
    seconds = [
        (2.0 / (2.0 - error)) * dot(x, e.astype(bf16))
        for x, e, error in zip(narrow, defects, errors)
    ]
    wide = [x.astype(bf16) for x in seconds]
    rests = [identity - dot_both(p, x) for p, x in zip(parts, wide)]
    small = [r.astype(bf16) for r in rests]
    sums = [r + dot(s, s) for r, s in zip(rests, small)]
    inverses = [x.astype(f32) + dot(x, s.astype(bf16)) for x, s in zip(wide, sums)]
    return inverses, ratios


def traces_of(field, gather):
    high, middle, low = thirds(field)
    stacked = jnp.concatenate([high.astype(f32), middle.astype(f32), low.astype(f32)], axis=0)
    out = dot(stacked.astype(bf16), gather)
    return out[0:8] + (out[8:16] + out[16:24])


def at_even(axis):
    return lax.rem(lax.axis_index(axis), 2) == 0


def store_traces(traces, refs):
    for d, axis in enumerate(AXES):
        even = at_even(axis)
        lower = traces[:, 2 * LANES * d : 2 * LANES * d + LANES]
        upper = traces[:, 2 * LANES * d + LANES : 2 * LANES * (d + 1)]
        refs[2 * d][...] = jnp.where(even, upper, lower)
        refs[2 * d + 1][...] = jnp.where(even, lower, upper)


def apply_inverses(inverse_ref, columns):
    rows = []
    for e in range(CELLS):
        rows.append(jnp.sum(inverse_ref[e] * columns[:, e : e + 1], axis=0, keepdims=True))
    return jnp.concatenate(rows, axis=0)


def rows_of(ref):
    return jnp.concatenate([ref[y] for y in range(ref.shape[0])], axis=0)


def invert_kernel(
    factor_ref, mass_ref, flags_ref, residual_ref, gather_hbm, wall_hbm, sides_hbm,
    inverse_ref, walls_ref, opens_ref, columns_ref, field_ref, *refs
):
    trace_refs, (wall_ref, sides_ref, gather_ref, sems) = refs[:6], refs[6:]
    targets = (wall_ref, sides_ref, gather_ref)
    loads = [
        pltpu.make_async_copy(source, target, sems.at[k])
        for k, (source, target) in enumerate(zip((wall_hbm, sides_hbm, gather_hbm), targets))
    ]
    for load in loads:
        load.start()
    masses = rows_of(mass_ref)
    columns = rows_of(residual_ref).T
    columns_ref[...] = columns
    lows = []
    heads, crosses, backs, tails = [], [], [], []
    for e in range(CELLS):
        factor = factor_ref[e]
        factor_t = factor.T
        scale = 1.0 / UNKNOWNS
        mass = masses[e : e + 1, :]
        lows.append(jnp.min(mass, axis=1, keepdims=True))
        left = scale * dot(factor_t, factor[:, :HEAD])
        right = scale * dot(factor_t, factor[:, HEAD:])
        heads.append(left[:HEAD] + jnp.where(eye_mask(HEAD), mass[:, :HEAD], 0.0))
        backs.append(left[HEAD:])
        crosses.append(right[:HEAD])
        tails.append(right[HEAD:] + jnp.where(eye_mask(TAIL), mass[:, HEAD:], 0.0))
    firsts, ratios = approximate_inverses(heads, lows)
    first_parts = [halves(x) for x in firsts]
    carried = [dot_split(p, halves(c)) for p, c in zip(first_parts, crosses)]
    carried_parts = [halves(c) for c in carried]
    schurs = [
        tail - dot_split(halves(back), c) for tail, back, c in zip(tails, backs, carried_parts)
    ]
    lasts, more = approximate_inverses(schurs, lows)
    last_parts = [halves(x) for x in lasts]
    for e in range(CELLS):
        corner = -dot_split(carried_parts[e], last_parts[e])
        inverse_ref[e, HEAD:, HEAD:] = lasts[e]
        inverse_ref[e, :HEAD, HEAD:] = corner
        inverse_ref[e, HEAD:, :HEAD] = corner.T
        inverse_ref[e, :HEAD, :HEAD] = firsts[e] - dot_split_nt(halves(corner), carried_parts[e])
    worst = ratios[0]
    for ratio in ratios[1:] + more:
        worst = jnp.maximum(worst, ratio)

    @pl.when(jnp.logical_not(jnp.max(worst) <= CONDITION_LIMIT))
    def _():
        diagonal = eye_mask(UNKNOWNS)
        lane = lax.broadcasted_iota(jnp.int32, (1, UNKNOWNS), 1)
        line = lax.broadcasted_iota(jnp.int32, (UNKNOWNS, 1), 0)

        def element(e, carry):
            factor = factor_ref[e]
            line8 = lax.broadcasted_iota(jnp.int32, (CELLS, 1), 0)
            mass = jnp.sum(jnp.where(line8 == e, masses, 0.0), axis=0, keepdims=True)
            inverse_ref[e] = dot(factor.T, factor) / UNKNOWNS + jnp.where(diagonal, mass, 0.0)

            def sweep(k, inner):
                table = inverse_ref[e]
                row = inverse_ref[e, pl.ds(k, 1), :]
                column = jnp.sum(jnp.where(diagonal, row, 0.0), axis=1, keepdims=True)
                pivot = jnp.sum(jnp.where(lane == k, row, 0.0), axis=1, keepdims=True)
                scaled = row / pivot
                swept = table - column * scaled
                swept = jnp.where(line == k, scaled, swept)
                swept = jnp.where(lane == k, column / pivot, swept)
                swept = jnp.where((line == k) & (lane == k), -1.0 / pivot, swept)
                inverse_ref[e] = swept
                return inner

            lax.fori_loop(0, UNKNOWNS, sweep, 0)
            inverse_ref[e] = -inverse_ref[e]
            return carry

        lax.fori_loop(0, CELLS, element, 0)

    field = apply_inverses(inverse_ref, columns)
    field_ref[...] = field
    for load in loads:
        load.wait()
    flags = rows_of(flags_ref).astype(f32).astype(bf16)
    walls_ref[...] = wall_weight * dot(flags, wall_ref[...])
    open_sides = 1.0 - dot_nt(sides_ref[...], flags)
    side_lane = lax.broadcasted_iota(jnp.int32, (FACE, CELLS), 1)
    for d, axis in enumerate(AXES):
        step, count = STEPS[d], COUNTS[d]
        has_above = lax.axis_index(axis) < lax.axis_size(axis) - 1
        at_top = (side_lane // step) % count == count - 1
        opens_ref[2 * d * FACE : (2 * d + 1) * FACE] = -open_sides[2 * d * FACE : (2 * d + 1) * FACE]
        opens_ref[(2 * d + 1) * FACE : (2 * d + 2) * FACE] = jnp.where(
            jnp.logical_and(at_top, jnp.logical_not(has_above)),
            0.0,
            open_sides[(2 * d + 1) * FACE : (2 * d + 2) * FACE],
        )
    store_traces(traces_of(field, gather_ref[...]), trace_refs)


def widened(trace):
    return jnp.concatenate([trace, jnp.zeros_like(trace)], axis=1)


def coupled(
    field_ref, walls_ref, opens_ref, face_ref, tops, own, received, scatter_ref
):
    lane8 = lax.broadcasted_iota(jnp.int32, (FACE, CELLS), 1)
    pieces = []
    for d, axis in enumerate(AXES):
        here = lax.axis_index(axis)
        has_below = here > 0
        even = at_even(axis)
        sent, got = own[2 * d : 2 * d + 2], received[2 * d : 2 * d + 2]
        lower = jnp.where(even, sent[1][...], sent[0][...])
        lower = pltpu.roll(widened(lower), FACE, 1)
        upper = widened(jnp.where(even, sent[0][...], sent[1][...]))
        below = jnp.where(even, got[1][...], got[0][...])
        below = widened(jnp.where(has_below, below, 0.0))
        above = jnp.where(even, got[0][...], got[1][...])
        above = pltpu.roll(widened(above), FACE, 1)
        step, count = STEPS[d], COUNTS[d]
        faces = CELLS // count
        rest = above[:, LANES:]
        rests = [rest] + [pltpu.roll(rest, 32 * k, 1) for k in range(1, min(faces, 4))]
        low_part = jnp.zeros((FACE, CELLS), f32)
        high_part = jnp.zeros((FACE, CELLS), f32)
        for e in range(CELLS):
            spot = (e // step) % count
            if spot == 0:
                other = e + step * (count - 1)
                left = below[other : other + 1]
            else:
                left = upper[e - step : e - step + 1]
            pair = left + lower[e : e + 1]
            flux = jnp.sum(face_ref[e, d] * pair[:, : 2 * FACE], axis=1, keepdims=True)
            low_part = jnp.where(lane8 == e, flux, low_part)
            if spot > 0:
                high_part = jnp.where(lane8 == e - step, flux, high_part)
            if spot == count - 1:
                first = e - step * (count - 1)
                slot = (e, e - 6, e // 2)[d]
                pair = upper[e : e + 1, :LANES] + above[first : first + 1, :LANES]
                tail = rests[slot % 4][first : first + 1]
                flux = jnp.sum(
                    tops[d][slot] * pair + tops[d][faces + slot // 4] * tail, axis=1, keepdims=True
                )
                high_part = jnp.where(lane8 == e, flux, high_part)
        pieces += [low_part, high_part]
    flux_columns = opens_ref[...] * jnp.concatenate(pieces, axis=0)
    scatter = scatter_ref[...]
    high, middle, low = thirds(flux_columns)
    columns = dot(scatter, high) + (dot(scatter, middle) + dot(scatter, low))
    return columns + (walls_ref[...] * field_ref[...]).T


def split_refs(refs):
    own, received, tops = refs[:6], refs[6:12], refs[12:15]
    return own, received, tops, refs[15:]


def step_kernel(inverse_ref, walls_ref, opens_ref, gather_ref, scatter_ref, field_ref, face_ref, *refs):
    own, received, tops, outs = split_refs(refs)
    columns = coupled(field_ref, walls_ref, opens_ref, face_ref, tops, own, received, scatter_ref)
    outs[0][...] = columns
    field = apply_inverses(inverse_ref, columns)
    outs[1][...] = field
    store_traces(traces_of(field, gather_ref[...]), outs[2:])


def dots_kernel(walls_ref, opens_ref, scatter_ref, field_ref, face_ref, first_ref, second_ref, third_ref, *refs):
    own, received, tops, outs = split_refs(refs)
    last = coupled(field_ref, walls_ref, opens_ref, face_ref, tops, own, received, scatter_ref)
    vectors = [first_ref[...], second_ref[...], third_ref[...], last]
    lane = lax.broadcasted_iota(jnp.int32, (8, LANES), 1)
    packed = jnp.zeros((8, LANES), f32)
    for i in range(4):
        for j in range(i, 4):
            value = jnp.sum(jnp.sum(vectors[i] * vectors[j], axis=0, keepdims=True), axis=1, keepdims=True)
            packed = jnp.where(lane == 4 * i + j, value, packed)
    outs[0][...] = packed


def least_squares(columns, start_norm):
    count = len(columns)
    cosines = []
    sine_terms = []
    target_values = [start_norm] + [jnp.zeros_like(start_norm) for i in range(count)]
    triangle = []
    for j in range(count):
        column = list(columns[j])
        for i in range(j):
            first_entry = column[i]
            second_entry = column[i + 1]
            column[i] = cosines[i] * first_entry + sine_terms[i] * second_entry
            column[i + 1] = -sine_terms[i] * first_entry + cosines[i] * second_entry
        radius = jnp.sqrt(column[j] * column[j] + column[j + 1] * column[j + 1])
        cosine = column[j] / radius
        sine_part = column[j + 1] / radius
        cosines.append(cosine)
        sine_terms.append(sine_part)
        column[j] = radius
        target_values[j + 1] = -sine_part * target_values[j]
        target_values[j] = cosine * target_values[j]
        triangle.append(column[: j + 1])
    weights = [None] * count
    for i in reversed(range(count)):
        running = target_values[i]
        for k in range(i + 1, count):
            running = running - triangle[k][i] * weights[k]
        weights[i] = running / triangle[i][i]
    return weights


def finish_kernel(partial_ref, first_ref, second_ref, third_ref, out_ref):
    totals = jnp.sum(partial_ref[...], axis=0, keepdims=True)
    lane = lax.broadcasted_iota(jnp.int32, (1, LANES), 1)

    def entry(i, j):
        return jnp.sum(jnp.where(lane == 4 * i + j, totals, 0.0), axis=1, keepdims=True)

    upper = [[None] * 4 for i in range(4)]
    for i in range(4):
        for j in range(i, 4):
            value = entry(i, j)
            for k in range(i):
                value = value - upper[k][i] * upper[k][j]
            upper[i][j] = jnp.sqrt(value) if i == j else value / upper[i][i]
    columns = []
    for j in range(KRYLOV):
        column = []
        for i in range(j + 2):
            value = upper[i][j + 1]
            if i <= j:
                value = value + upper[i][j]
            column.append(value)
        columns.append(column)
    weights = least_squares(columns, upper[0][0])
    update = weights[0] * first_ref[...] + weights[1] * second_ref[...] + weights[2] * third_ref[...]
    for y in range(COUNTS[1]):
        out_ref[y] = update[2 * y : 2 * y + 2]


def vmem(count):
    return [pl.BlockSpec(memory_space=pltpu.VMEM)] * count


TOPS = [(e, 0) for e in range(CELLS)] + [(0, 1), (1, 1)] + [(e, 2) for e in (0, 2, 4, 6)]


def slabs_kernel(face_hbm, factor_hbm, mass_hbm, flags_hbm, residual_hbm, *refs):
    outs, kept, (slab_ref, sems) = refs[:3], refs[3:7], refs[7:]
    loads = []
    for slot, (e, d) in enumerate(TOPS):
        loads.append(pltpu.make_async_copy(face_hbm.at[e, d], slab_ref.at[slot], sems.at[slot]))
        loads[-1].start()
    others = []
    for k, (source, target) in enumerate(zip((factor_hbm, mass_hbm, flags_hbm, residual_hbm), kept)):
        others.append(pltpu.make_async_copy(source, target, sems.at[len(TOPS) + k]))
        others[-1].start()
    for load in loads:
        load.wait()
    for d, (start, count) in enumerate(((0, CELLS), (CELLS, 2), (CELLS + 2, 4))):
        out = outs[d]
        for slot in range(count):
            out[slot] = slab_ref[start + slot, :, :LANES]
        for first in range(0, count, 4):
            group = [
                slab_ref[start + slot, :, LANES:] for slot in range(first, min(first + 4, count))
            ]
            if len(group) < 4:
                group.append(jnp.zeros((FACE, LANES - 32 * len(group)), f32))
            out[count + first // 4] = jnp.concatenate(group, axis=1)
    for load in others:
        load.wait()


HBM_SPEC = pl.BlockSpec(memory_space=pltpu.HBM)


def call(kernel, specs, shapes, name, megabytes, args, scratch=()):
    args = [
        pltpu.with_memory_space_constraint(arg, pltpu.HBM) if spec is HBM_SPEC else arg
        for arg, spec in zip(args, specs)
    ]
    return pl.pallas_call(
        kernel,
        out_shape=[
            shape if isinstance(shape, jax.ShapeDtypeStruct) else jax.ShapeDtypeStruct(shape, f32)
            for shape in shapes
        ],
        in_specs=specs,
        out_specs=vmem(len(shapes)),
        scratch_shapes=scratch,
        name=name,
        compiler_params=pltpu.CompilerParams(vmem_limit_bytes=megabytes << 20),
    )(*args)


TRACE_SHAPES = [(CELLS, LANES)] * 6
INVERT_SHAPES = [
    (CELLS, UNKNOWNS, UNKNOWNS),
    (CELLS, UNKNOWNS),
    (6 * FACE, CELLS),
    (UNKNOWNS, CELLS),
    (CELLS, UNKNOWNS),
] + TRACE_SHAPES
INVERT_SCRATCH = [
    pltpu.VMEM((6, UNKNOWNS), bf16),
    pltpu.VMEM((6 * FACE, 6), bf16),
    pltpu.VMEM((UNKNOWNS, 6 * LANES), bf16),
    pltpu.SemaphoreType.DMA((3,)),
]
SLAB_SHAPES = [(10, FACE, LANES), (3, FACE, LANES), (5, FACE, LANES)]


def around(block, axis, distance):
    count = lax.axis_size(axis)
    return lax.ppermute(block, axis, [(i, (i + distance) % count) for i in range(count)])


def exchanged(own):
    received = []
    for d, axis in enumerate(AXES):
        count = lax.axis_size(axis)
        pairs = [(i, i ^ 1) for i in range(count)]
        received.append(lax.ppermute(own[2 * d], axis, pairs))
        pairs = [(i, (((i + 1) ^ 1) - 1) % count) for i in range(count)]
        received.append(lax.ppermute(own[2 * d + 1], axis, pairs))
    return received


def shards(flux_jacobian_factor, mass_over_timestep, face_jacobian, face_flags, right_side):
    gather = jnp.asarray(gather_matrix(), bf16)
    scatter = jnp.asarray(scatter_matrix(), bf16)
    wall = jnp.asarray(wall_table(), bf16)
    sides = jnp.asarray(side_table(), bf16)
    faces = face_jacobian.reshape(CELLS, 3, FACE, 2 * FACE)
    operands = (
        flux_jacobian_factor.reshape(CELLS, UNKNOWNS, UNKNOWNS),
        mass_over_timestep.reshape(4, 2, UNKNOWNS),
        face_flags.reshape(4, 2, 6),
        right_side.reshape(4, 2, UNKNOWNS),
    )
    *slabs, factor, mass, flags, residual = call(
        slabs_kernel,
        [HBM_SPEC] * 5,
        SLAB_SHAPES + [jax.ShapeDtypeStruct(a.shape, a.dtype) for a in operands],
        "slabs",
        8,
        (faces, *operands),
        [pltpu.VMEM((len(TOPS), FACE, 2 * FACE), f32), pltpu.SemaphoreType.DMA((len(TOPS) + 4,))],
    )
    tops = [around(slab, axis, -1) for slab, axis in zip(slabs, AXES)]
    inverse, walls, opens, columns, field, *own = call(
        invert_kernel,
        vmem(4) + [HBM_SPEC] * 3,
        INVERT_SHAPES,
        "invert",
        INVERT_MIB,
        (factor, mass, flags, residual, gather, wall, sides),
        INVERT_SCRATCH,
    )
    vectors, fields = [columns], [field]
    for j in range(KRYLOV - 1):
        received = exchanged(own)
        columns, field, *own = call(
            step_kernel,
            vmem(22),
            [(UNKNOWNS, CELLS), (CELLS, UNKNOWNS)] + TRACE_SHAPES,
            "step",
            STEP_MIB,
            (inverse, walls, opens, gather, scatter, fields[j], faces, *own, *received, *tops),
        )
        vectors.append(columns)
        fields.append(field)
    received = exchanged(own)
    (packed,) = call(
        dots_kernel,
        vmem(23),
        [(8, LANES)],
        "dots",
        STEP_MIB,
        (walls, opens, scatter, fields[2], faces, *vectors, *own, *received, *tops),
    )
    devices = lax.axis_size("gx") * lax.axis_size("gy") * lax.axis_size("gz")
    spread = jnp.broadcast_to(packed[0:1], (devices, LANES))
    partial = lax.all_to_all(spread, AXES, 0, 0, tiled=True)
    (update,) = call(
        finish_kernel, vmem(4), [(4, 2, UNKNOWNS)], "finish", 8, (partial, *fields)
    )
    return update.reshape(right_side.shape)


def solution(mesh):
    in_specs = (
        P("gx", "gy", "gz", None, None),
        P("gx", "gy", "gz", None),
        P("gx", "gy", "gz", None, None, None),
        P("gx", "gy", "gz", None),
        P("gx", "gy", "gz", None),
    )
    out_specs = P("gx", "gy", "gz", None)
    return jax.shard_map(shards, mesh=mesh, in_specs=in_specs, out_specs=out_specs, check_vma=False)
```

```python
import jax
import jax.numpy as jnp
import numpy as np
from jax import lax
from jax.experimental import pallas as pl
from jax.experimental.pallas import tpu as pltpu
from jax.sharding import PartitionSpec as P

VARS = 5
ORDER = 4
KRYLOV = 3
UNKNOWNS = 320
FACE = 80
HEAD = 128
TAIL = UNKNOWNS - HEAD
CELLS = 8
LANES = 128
CONDITION_LIMIT = 26.0
wall_weight = 0.5
INVERT_MIB = 28
STEP_MIB = 16


f32 = jnp.float32
bf16 = jnp.bfloat16
AXES = ("gx", "gy", "gz")
COUNTS = (1, 4, 2)
STEPS = (CELLS, 2, 1)


def face_nodes():
    cube = np.arange(UNKNOWNS).reshape(VARS, ORDER, ORDER, ORDER)
    nodes = []
    for d in range(3):
        for index in (0, ORDER - 1):
            nodes.append(np.take(cube, index, axis=1 + d).reshape(-1))
    return nodes


def gather_matrix():
    table = np.zeros((UNKNOWNS, 6 * LANES), np.float32)
    for side, nodes in enumerate(face_nodes()):
        for k in range(FACE):
            table[nodes[k], LANES * side + k] = 1.0
    return table


def scatter_matrix():
    table = np.zeros((UNKNOWNS, 6 * FACE), np.float32)
    for side, nodes in enumerate(face_nodes()):
        for k in range(FACE):
            table[nodes[k], FACE * side + k] = 1.0
    return table


def side_table():
    return np.repeat(np.eye(6, dtype=np.float32), FACE, axis=0)


def wall_table():
    table = np.zeros((6, UNKNOWNS), np.float32)
    for side, nodes in enumerate(face_nodes()):
        table[side, nodes] = 1.0
    return table


def dot(a, b):
    return jnp.dot(a, b, preferred_element_type=f32)


def dot_nt(a, b):
    return lax.dot_general(a, b, (((1,), (1,)), ((), ())), preferred_element_type=f32)


def halves(a):
    high = a.astype(bf16)
    return high, (a - high.astype(f32)).astype(bf16)


def thirds(a):
    high = a.astype(bf16)
    rest = a - high.astype(f32)
    middle = rest.astype(bf16)
    return high, middle, (rest - middle.astype(f32)).astype(bf16)


def dot_both(a, b):
    rows = a[0].shape[0]
    both = dot(jnp.concatenate(a, axis=0), b)
    return both[:rows] + both[rows:]


def dot_split(a, b):
    return dot_both(a, b[0]) + dot(a[0], b[1])


def dot_split_nt(a, b):
    rows = a[0].shape[0]
    both = dot_nt(jnp.concatenate(a, axis=0), b[0])
    return both[:rows] + (both[rows:] + dot_nt(a[0], b[1]))


def eye_mask(n):
    rows = lax.broadcasted_iota(jnp.int32, (n, n), 0)
    cols = lax.broadcasted_iota(jnp.int32, (n, n), 1)
    return rows == cols


def approximate_inverses(blocks, lows):
    n = blocks[0].shape[0]
    diagonal = eye_mask(n)
    identity = jnp.where(diagonal, 1.0, 0.0)
    parts = [halves(a) for a in blocks]
    squares = [dot(p[0], p[0]) for p in parts]
    firsts, errors, ratios = [], [], []
    for a, square, low in zip(blocks, squares, lows):
        sums = jnp.sum(jnp.abs(square), axis=0, keepdims=True)
        high = 1.03 * jnp.sqrt(jnp.max(sums, axis=1, keepdims=True))
        high = jnp.maximum(high, 1.1 * low)
        ratios.append(high / low)
        half = 0.5 * (high - low)
        scale = 1.0 / half
        t = -0.5 * (high + low) * scale
        t2 = t * t
        c3 = 16.0 * t
        c2 = 16.0 * t2 - 20.0
        c1 = t * c2
        c0 = t2 * c2 + 5.0
        top = t * c0
        gain = -scale / top
        square_scale = scale * scale
        slope = 2.0 * t * scale
        inner_slope = c3 * scale + 16.0 * slope
        both = c3 * t + 16.0 * t2
        outer = square_scale * square + slope * a
        inner = (16.0 * gain * square_scale) * square + (gain * inner_slope) * a
        by_square = gain * square_scale * (16.0 * t2 + both + c2)
        by_a = gain * (t2 * inner_slope + both * slope + c1 * scale + c2 * slope)
        by_one = gain * (t2 * both + c1 * t + c2 * t2 + c0)
        base = by_square * square + by_a * a + by_one * identity
        firsts.append(base + dot(outer.astype(bf16), inner.astype(bf16)))
        errors.append(1.0 / (top * top))
    narrow = [x.astype(bf16) for x in firsts]
    defects = [2.0 * identity - dot(p[0], x) for p, x in zip(parts, narrow)]
    seconds = [
        (2.0 / (2.0 - error)) * dot(x, e.astype(bf16))
        for x, e, error in zip(narrow, defects, errors)
    ]
    wide = [x.astype(bf16) for x in seconds]
    rests = [identity - dot_both(p, x) for p, x in zip(parts, wide)]
    small = [r.astype(bf16) for r in rests]
    sums = [r + dot(s, s) for r, s in zip(rests, small)]
    inverses = [x.astype(f32) + dot(x, s.astype(bf16)) for x, s in zip(wide, sums)]
    return inverses, ratios


def traces_of(field, gather):
    high, middle, low = thirds(field)
    stacked = jnp.concatenate([high.astype(f32), middle.astype(f32), low.astype(f32)], axis=0)
    out = dot(stacked.astype(bf16), gather)
    return out[0:8] + (out[8:16] + out[16:24])


def at_even(axis):
    return lax.rem(lax.axis_index(axis), 2) == 0


def store_traces(traces, refs):
    for d, axis in enumerate(AXES):
        even = at_even(axis)
        lower = traces[:, 2 * LANES * d : 2 * LANES * d + LANES]
        upper = traces[:, 2 * LANES * d + LANES : 2 * LANES * (d + 1)]
        refs[2 * d][...] = jnp.where(even, upper, lower)
        refs[2 * d + 1][...] = jnp.where(even, lower, upper)


def apply_inverses(inverse_ref, columns):
    rows = []
    for e in range(CELLS):
        rows.append(jnp.sum(inverse_ref[e] * columns[:, e : e + 1], axis=0, keepdims=True))
    return jnp.concatenate(rows, axis=0)


def rows_of(ref):
    return jnp.concatenate([ref[y] for y in range(ref.shape[0])], axis=0)


def invert_kernel(
    factor_ref, mass_ref, flags_ref, residual_ref, gather_hbm, wall_hbm, sides_hbm,
    inverse_ref, walls_ref, opens_ref, columns_ref, field_ref, *refs
):
    trace_refs, (wall_ref, sides_ref, gather_ref, sems) = refs[:6], refs[6:]
    targets = (wall_ref, sides_ref, gather_ref)
    loads = [
        pltpu.make_async_copy(source, target, sems.at[k])
        for k, (source, target) in enumerate(zip((wall_hbm, sides_hbm, gather_hbm), targets))
    ]
    for load in loads:
        load.start()
    masses = rows_of(mass_ref)
    columns = rows_of(residual_ref).T
    columns_ref[...] = columns
    lows = []
    heads, crosses, backs, tails = [], [], [], []
    for e in range(CELLS):
        factor = factor_ref[e]
        factor_t = factor.T
        scale = 1.0 / UNKNOWNS
        mass = masses[e : e + 1, :]
        lows.append(jnp.min(mass, axis=1, keepdims=True))
        left = scale * dot(factor_t, factor[:, :HEAD])
        right = scale * dot(factor_t, factor[:, HEAD:])
        heads.append(left[:HEAD] + jnp.where(eye_mask(HEAD), mass[:, :HEAD], 0.0))
        backs.append(left[HEAD:])
        crosses.append(right[:HEAD])
        tails.append(right[HEAD:] + jnp.where(eye_mask(TAIL), mass[:, HEAD:], 0.0))
    firsts, ratios = approximate_inverses(heads, lows)
    first_parts = [halves(x) for x in firsts]
    carried = [dot_split(p, halves(c)) for p, c in zip(first_parts, crosses)]
    carried_parts = [halves(c) for c in carried]
    schurs = [
        tail - dot_split(halves(back), c) for tail, back, c in zip(tails, backs, carried_parts)
    ]
    lasts, more = approximate_inverses(schurs, lows)
    last_parts = [halves(x) for x in lasts]
    for e in range(CELLS):
        corner = -dot_split(carried_parts[e], last_parts[e])
        inverse_ref[e, HEAD:, HEAD:] = lasts[e]
        inverse_ref[e, :HEAD, HEAD:] = corner
        inverse_ref[e, HEAD:, :HEAD] = corner.T
        inverse_ref[e, :HEAD, :HEAD] = firsts[e] - dot_split_nt(halves(corner), carried_parts[e])
    worst = ratios[0]
    for ratio in ratios[1:] + more:
        worst = jnp.maximum(worst, ratio)

    @pl.when(jnp.logical_not(jnp.max(worst) <= CONDITION_LIMIT))
    def _():
        diagonal = eye_mask(UNKNOWNS)
        lane = lax.broadcasted_iota(jnp.int32, (1, UNKNOWNS), 1)
        line = lax.broadcasted_iota(jnp.int32, (UNKNOWNS, 1), 0)

        def element(e, carry):
            factor = factor_ref[e]
            line8 = lax.broadcasted_iota(jnp.int32, (CELLS, 1), 0)
            mass = jnp.sum(jnp.where(line8 == e, masses, 0.0), axis=0, keepdims=True)
            inverse_ref[e] = dot(factor.T, factor) / UNKNOWNS + jnp.where(diagonal, mass, 0.0)

            def sweep(k, inner):
                table = inverse_ref[e]
                row = inverse_ref[e, pl.ds(k, 1), :]
                column = jnp.sum(jnp.where(diagonal, row, 0.0), axis=1, keepdims=True)
                pivot = jnp.sum(jnp.where(lane == k, row, 0.0), axis=1, keepdims=True)
                scaled = row / pivot
                swept = table - column * scaled
                swept = jnp.where(line == k, scaled, swept)
                swept = jnp.where(lane == k, column / pivot, swept)
                swept = jnp.where((line == k) & (lane == k), -1.0 / pivot, swept)
                inverse_ref[e] = swept
                return inner

            lax.fori_loop(0, UNKNOWNS, sweep, 0)
            inverse_ref[e] = -inverse_ref[e]
            return carry

        lax.fori_loop(0, CELLS, element, 0)

    field = apply_inverses(inverse_ref, columns)
    field_ref[...] = field
    for load in loads:
        load.wait()
    flags = rows_of(flags_ref).astype(f32).astype(bf16)
    walls_ref[...] = wall_weight * dot(flags, wall_ref[...])
    open_sides = 1.0 - dot_nt(sides_ref[...], flags)
    side_lane = lax.broadcasted_iota(jnp.int32, (FACE, CELLS), 1)
    for d, axis in enumerate(AXES):
        step, count = STEPS[d], COUNTS[d]
        has_above = lax.axis_index(axis) < lax.axis_size(axis) - 1
        at_top = (side_lane // step) % count == count - 1
        opens_ref[2 * d * FACE : (2 * d + 1) * FACE] = -open_sides[2 * d * FACE : (2 * d + 1) * FACE]
        opens_ref[(2 * d + 1) * FACE : (2 * d + 2) * FACE] = jnp.where(
            jnp.logical_and(at_top, jnp.logical_not(has_above)),
            0.0,
            open_sides[(2 * d + 1) * FACE : (2 * d + 2) * FACE],
        )
    store_traces(traces_of(field, gather_ref[...]), trace_refs)


def widened(trace):
    return jnp.concatenate([trace, jnp.zeros_like(trace)], axis=1)


def coupled(
    field_ref, walls_ref, opens_ref, face_ref, tops, own, received, scatter_ref
):
    lane8 = lax.broadcasted_iota(jnp.int32, (FACE, CELLS), 1)
    pieces = []
    for d, axis in enumerate(AXES):
        here = lax.axis_index(axis)
        has_below = here > 0
        even = at_even(axis)
        sent, got = own[2 * d : 2 * d + 2], received[2 * d : 2 * d + 2]
        lower = jnp.where(even, sent[1][...], sent[0][...])
        lower = pltpu.roll(widened(lower), FACE, 1)
        upper = widened(jnp.where(even, sent[0][...], sent[1][...]))
        below = jnp.where(even, got[1][...], got[0][...])
        below = widened(jnp.where(has_below, below, 0.0))
        above = jnp.where(even, got[0][...], got[1][...])
        above = pltpu.roll(widened(above), FACE, 1)
        step, count = STEPS[d], COUNTS[d]
        faces = CELLS // count
        rest = above[:, LANES:]
        rests = [rest] + [pltpu.roll(rest, 32 * k, 1) for k in range(1, min(faces, 4))]
        low_part = jnp.zeros((FACE, CELLS), f32)
        high_part = jnp.zeros((FACE, CELLS), f32)
        for e in range(CELLS):
            spot = (e // step) % count
            if spot == 0:
                other = e + step * (count - 1)
                left = below[other : other + 1]
            else:
                left = upper[e - step : e - step + 1]
            pair = left + lower[e : e + 1]
            flux = jnp.sum(face_ref[e, d] * pair[:, : 2 * FACE], axis=1, keepdims=True)
            low_part = jnp.where(lane8 == e, flux, low_part)
            if spot > 0:
                high_part = jnp.where(lane8 == e - step, flux, high_part)
            if spot == count - 1:
                first = e - step * (count - 1)
                slot = (e, e - 6, e // 2)[d]
                pair = upper[e : e + 1, :LANES] + above[first : first + 1, :LANES]
                tail = rests[slot % 4][first : first + 1]
                flux = jnp.sum(
                    tops[d][slot] * pair + tops[d][faces + slot // 4] * tail, axis=1, keepdims=True
                )
                high_part = jnp.where(lane8 == e, flux, high_part)
        pieces += [low_part, high_part]
    flux_columns = opens_ref[...] * jnp.concatenate(pieces, axis=0)
    scatter = scatter_ref[...]
    high, middle, low = thirds(flux_columns)
    columns = dot(scatter, high) + (dot(scatter, middle) + dot(scatter, low))
    return columns + (walls_ref[...] * field_ref[...]).T


def split_refs(refs):
    own, received, tops = refs[:6], refs[6:12], refs[12:15]
    return own, received, tops, refs[15:]


def step_kernel(inverse_ref, walls_ref, opens_ref, gather_ref, scatter_ref, field_ref, face_ref, *refs):
    own, received, tops, outs = split_refs(refs)
    columns = coupled(field_ref, walls_ref, opens_ref, face_ref, tops, own, received, scatter_ref)
    outs[0][...] = columns
    field = apply_inverses(inverse_ref, columns)
    outs[1][...] = field
    store_traces(traces_of(field, gather_ref[...]), outs[2:])


def dots_kernel(walls_ref, opens_ref, scatter_ref, field_ref, face_ref, first_ref, second_ref, third_ref, *refs):
    own, received, tops, outs = split_refs(refs)
    last = coupled(field_ref, walls_ref, opens_ref, face_ref, tops, own, received, scatter_ref)
    vectors = [first_ref[...], second_ref[...], third_ref[...], last]
    lane = lax.broadcasted_iota(jnp.int32, (8, LANES), 1)
    packed = jnp.zeros((8, LANES), f32)
    for i in range(4):
        for j in range(i, 4):
            value = jnp.sum(jnp.sum(vectors[i] * vectors[j], axis=0, keepdims=True), axis=1, keepdims=True)
            packed = jnp.where(lane == 4 * i + j, value, packed)
    outs[0][...] = packed


def least_squares(columns, start_norm):
    count = len(columns)
    cosines = []
    sine_terms = []
    target_values = [start_norm] + [jnp.zeros_like(start_norm) for i in range(count)]
    triangle = []
    for j in range(count):
        column = list(columns[j])
        for i in range(j):
            first_entry = column[i]
            second_entry = column[i + 1]
            column[i] = cosines[i] * first_entry + sine_terms[i] * second_entry
            column[i + 1] = -sine_terms[i] * first_entry + cosines[i] * second_entry
        radius = jnp.sqrt(column[j] * column[j] + column[j + 1] * column[j + 1])
        used = radius > 0.0
        divisor = jnp.where(used, radius, 1.0)
        cosine = jnp.where(used, column[j] / divisor, 1.0)
        sine_part = jnp.where(used, column[j + 1] / divisor, 0.0)
        cosines.append(cosine)
        sine_terms.append(sine_part)
        column[j] = radius
        target_values[j + 1] = -sine_part * target_values[j]
        target_values[j] = cosine * target_values[j]
        triangle.append(column[: j + 1])
    weights = [None] * count
    for i in reversed(range(count)):
        running = target_values[i]
        for k in range(i + 1, count):
            running = running - triangle[k][i] * weights[k]
        used = triangle[i][i] > 0.0
        weights[i] = jnp.where(used, running / jnp.where(used, triangle[i][i], 1.0), 0.0)
    return weights


def finish_kernel(partial_ref, first_ref, second_ref, third_ref, out_ref):
    totals = jnp.sum(partial_ref[...], axis=0, keepdims=True)
    lane = lax.broadcasted_iota(jnp.int32, (1, LANES), 1)

    def entry(i, j):
        return jnp.sum(jnp.where(lane == 4 * i + j, totals, 0.0), axis=1, keepdims=True)

    upper = [[None] * 4 for i in range(4)]
    for i in range(4):
        for j in range(i, 4):
            square = entry(i, j)
            value = square
            for k in range(i):
                value = value - upper[k][i] * upper[k][j]
            if i == j:
                upper[i][i] = jnp.where(value > 1e-6 * square, jnp.sqrt(jnp.maximum(value, 0.0)), 0.0)
            else:
                used = upper[i][i] > 0.0
                upper[i][j] = jnp.where(used, value / jnp.where(used, upper[i][i], 1.0), 0.0)
    columns = []
    for j in range(KRYLOV):
        column = []
        for i in range(j + 2):
            value = upper[i][j + 1]
            if i <= j:
                value = value + upper[i][j]
            column.append(value)
        columns.append(column)
    weights = least_squares(columns, upper[0][0])
    update = weights[0] * first_ref[...] + weights[1] * second_ref[...] + weights[2] * third_ref[...]
    for y in range(COUNTS[1]):
        out_ref[y] = update[2 * y : 2 * y + 2]


def vmem(count):
    return [pl.BlockSpec(memory_space=pltpu.VMEM)] * count


def slabs_kernel(face_hbm, factor_hbm, mass_hbm, flags_hbm, residual_hbm, *refs):
    outs, kept, (slab_ref, sems) = refs[:3], refs[3:7], refs[7:]
    pairs = [
        (face_hbm.at[:, 0], slab_ref.at[:CELLS]),
        (face_hbm.at[:2, 1], slab_ref.at[CELLS : CELLS + 2]),
    ]
    pairs += [(face_hbm.at[2 * k, 2], slab_ref.at[CELLS + 2 + k]) for k in range(4)]
    loads = []
    for k, (source, target) in enumerate(pairs):
        loads.append(pltpu.make_async_copy(source, target, sems.at[k]))
        loads[-1].start()
    others = []
    for k, (source, target) in enumerate(zip((factor_hbm, mass_hbm, flags_hbm, residual_hbm), kept)):
        others.append(pltpu.make_async_copy(source, target, sems.at[len(pairs) + k]))
        others[-1].start()
    for load in loads:
        load.wait()
    for d, (start, count) in enumerate(((0, CELLS), (CELLS, 2), (CELLS + 2, 4))):
        out = outs[d]
        for slot in range(count):
            out[slot] = slab_ref[start + slot, :, :LANES]
        for first in range(0, count, 4):
            group = [
                slab_ref[start + slot, :, LANES:] for slot in range(first, min(first + 4, count))
            ]
            if len(group) < 4:
                group.append(jnp.zeros((FACE, LANES - 32 * len(group)), f32))
            out[count + first // 4] = jnp.concatenate(group, axis=1)
    for load in others:
        load.wait()


HBM_SPEC = pl.BlockSpec(memory_space=pltpu.HBM)


def call(kernel, specs, shapes, name, megabytes, args, scratch=()):
    args = [
        pltpu.with_memory_space_constraint(arg, pltpu.HBM) if spec is HBM_SPEC else arg
        for arg, spec in zip(args, specs)
    ]
    return pl.pallas_call(
        kernel,
        out_shape=[
            shape if isinstance(shape, jax.ShapeDtypeStruct) else jax.ShapeDtypeStruct(shape, f32)
            for shape in shapes
        ],
        in_specs=specs,
        out_specs=vmem(len(shapes)),
        scratch_shapes=scratch,
        name=name,
        compiler_params=pltpu.CompilerParams(vmem_limit_bytes=megabytes << 20),
    )(*args)


TRACE_SHAPES = [(CELLS, LANES)] * 6
INVERT_SHAPES = [
    (CELLS, UNKNOWNS, UNKNOWNS),
    (CELLS, UNKNOWNS),
    (6 * FACE, CELLS),
    (UNKNOWNS, CELLS),
    (CELLS, UNKNOWNS),
] + TRACE_SHAPES
INVERT_SCRATCH = [
    pltpu.VMEM((6, UNKNOWNS), bf16),
    pltpu.VMEM((6 * FACE, 6), bf16),
    pltpu.VMEM((UNKNOWNS, 6 * LANES), bf16),
    pltpu.SemaphoreType.DMA((3,)),
]
SLAB_SHAPES = [(10, FACE, LANES), (3, FACE, LANES), (5, FACE, LANES)]


def around(block, axis, distance):
    count = lax.axis_size(axis)
    return lax.ppermute(block, axis, [(i, (i + distance) % count) for i in range(count)])


def exchanged(own):
    received = []
    for d, axis in enumerate(AXES):
        count = lax.axis_size(axis)
        pairs = [(i, i ^ 1) for i in range(count)]
        received.append(lax.ppermute(own[2 * d], axis, pairs))
        pairs = [(i, (((i + 1) ^ 1) - 1) % count) for i in range(count)]
        received.append(lax.ppermute(own[2 * d + 1], axis, pairs))
    return received


def shards(flux_jacobian_factor, mass_over_timestep, face_jacobian, face_flags, right_side):
    gather = jnp.asarray(gather_matrix(), bf16)
    scatter = jnp.asarray(scatter_matrix(), bf16)
    wall = jnp.asarray(wall_table(), bf16)
    sides = jnp.asarray(side_table(), bf16)
    faces = face_jacobian.reshape(CELLS, 3, FACE, 2 * FACE)
    operands = (
        flux_jacobian_factor.reshape(CELLS, UNKNOWNS, UNKNOWNS),
        mass_over_timestep.reshape(4, 2, UNKNOWNS),
        face_flags.reshape(4, 2, 6),
        right_side.reshape(4, 2, UNKNOWNS),
    )
    *slabs, factor, mass, flags, residual = call(
        slabs_kernel,
        [HBM_SPEC] * 5,
        SLAB_SHAPES + [jax.ShapeDtypeStruct(a.shape, a.dtype) for a in operands],
        "slabs",
        8,
        (faces, *operands),
        [pltpu.VMEM((14, FACE, 2 * FACE), f32), pltpu.SemaphoreType.DMA((10,))],
    )
    tops = [around(slab, axis, -1) for slab, axis in zip(slabs, AXES)]
    inverse, walls, opens, columns, field, *own = call(
        invert_kernel,
        vmem(4) + [HBM_SPEC] * 3,
        INVERT_SHAPES,
        "invert",
        INVERT_MIB,
        (factor, mass, flags, residual, gather, wall, sides),
        INVERT_SCRATCH,
    )
    vectors, fields = [columns], [field]
    for j in range(KRYLOV - 1):
        received = exchanged(own)
        columns, field, *own = call(
            step_kernel,
            vmem(22),
            [(UNKNOWNS, CELLS), (CELLS, UNKNOWNS)] + TRACE_SHAPES,
            "step",
            STEP_MIB,
            (inverse, walls, opens, gather, scatter, fields[j], faces, *own, *received, *tops),
        )
        vectors.append(columns)
        fields.append(field)
    received = exchanged(own)
    (packed,) = call(
        dots_kernel,
        vmem(23),
        [(8, LANES)],
        "dots",
        STEP_MIB,
        (walls, opens, scatter, fields[2], faces, *vectors, *own, *received, *tops),
    )
    devices = lax.axis_size("gx") * lax.axis_size("gy") * lax.axis_size("gz")
    spread = jnp.broadcast_to(packed[0:1], (devices, LANES))
    partial = lax.all_to_all(spread, AXES, 0, 0, tiled=True)
    (update,) = call(
        finish_kernel, vmem(4), [(4, 2, UNKNOWNS)], "finish", 8, (partial, *fields)
    )
    return update.reshape(right_side.shape)


def solution(mesh):
    in_specs = (
        P("gx", "gy", "gz", None, None),
        P("gx", "gy", "gz", None),
        P("gx", "gy", "gz", None, None, None),
        P("gx", "gy", "gz", None),
        P("gx", "gy", "gz", None),
    )
    out_specs = P("gx", "gy", "gz", None)
    return jax.shard_map(shards, mesh=mesh, in_specs=in_specs, out_specs=out_specs, check_vma=False)
```

```python
import jax
import jax.numpy as jnp
import numpy as np
from jax import lax
from jax.experimental import pallas as pl
from jax.experimental.pallas import tpu as pltpu
from jax.sharding import PartitionSpec as P

VARS = 5
ORDER = 4
KRYLOV = 3
UNKNOWNS = 320
FACE = 80
HEAD = 128
TAIL = UNKNOWNS - HEAD
CELLS = 8
LANES = 128
CONDITION_LIMIT = 26.0
wall_weight = 0.5
INVERT_MIB = 28
STEP_MIB = 16


f32 = jnp.float32
bf16 = jnp.bfloat16
AXES = ("gx", "gy", "gz")
COUNTS = (1, 4, 2)
STEPS = (CELLS, 2, 1)


def face_nodes():
    cube = np.arange(UNKNOWNS).reshape(VARS, ORDER, ORDER, ORDER)
    nodes = []
    for d in range(3):
        for index in (0, ORDER - 1):
            nodes.append(np.take(cube, index, axis=1 + d).reshape(-1))
    return nodes


def gather_matrix():
    table = np.zeros((UNKNOWNS, 6 * LANES), np.float32)
    for side, nodes in enumerate(face_nodes()):
        for k in range(FACE):
            table[nodes[k], LANES * side + k] = 1.0
    return table


def scatter_matrix():
    table = np.zeros((UNKNOWNS, 6 * FACE), np.float32)
    for side, nodes in enumerate(face_nodes()):
        for k in range(FACE):
            table[nodes[k], FACE * side + k] = 1.0
    return table


def side_table():
    return np.repeat(np.eye(6, dtype=np.float32), FACE, axis=0)


def wall_table():
    table = np.zeros((6, UNKNOWNS), np.float32)
    for side, nodes in enumerate(face_nodes()):
        table[side, nodes] = 1.0
    return table


def dot(a, b):
    return jnp.dot(a, b, preferred_element_type=f32)


def dot_nt(a, b):
    return lax.dot_general(a, b, (((1,), (1,)), ((), ())), preferred_element_type=f32)


def halves(a):
    high = a.astype(bf16)
    return high, (a - high.astype(f32)).astype(bf16)


def thirds(a):
    high = a.astype(bf16)
    rest = a - high.astype(f32)
    middle = rest.astype(bf16)
    return high, middle, (rest - middle.astype(f32)).astype(bf16)


def dot_both(a, b):
    rows = a[0].shape[0]
    both = dot(jnp.concatenate(a, axis=0), b)
    return both[:rows] + both[rows:]


def dot_split(a, b):
    return dot_both(a, b[0]) + dot(a[0], b[1])


def dot_split_nt(a, b):
    rows = a[0].shape[0]
    both = dot_nt(jnp.concatenate(a, axis=0), b[0])
    return both[:rows] + (both[rows:] + dot_nt(a[0], b[1]))


def eye_mask(n):
    rows = lax.broadcasted_iota(jnp.int32, (n, n), 0)
    cols = lax.broadcasted_iota(jnp.int32, (n, n), 1)
    return rows == cols


def approximate_inverses(blocks, lows):
    n = blocks[0].shape[0]
    diagonal = eye_mask(n)
    identity = jnp.where(diagonal, 1.0, 0.0)
    parts = [halves(a) for a in blocks]
    squares = [dot(p[0], p[0]) for p in parts]
    yield
    factors, errors, ratios = [], [], []
    for a, square, low in zip(blocks, squares, lows):
        sums = jnp.sum(jnp.abs(square), axis=0, keepdims=True)
        high = 1.03 * jnp.sqrt(jnp.max(sums, axis=1, keepdims=True))
        high = jnp.maximum(high, 1.1 * low)
        ratios.append(high / low)
        half = 0.5 * (high - low)
        scale = 1.0 / half
        t = -0.5 * (high + low) * scale
        t2 = t * t
        top = t * (t2 * (16.0 * t2 - 20.0) + 5.0)
        gain = -16.0 * scale / top
        quadratics = []
        for angle, weight in ((0.4 * np.pi, 1.0), (0.8 * np.pi, gain)):
            cosine, sine_square = float(np.cos(angle)), float(np.sin(angle) ** 2)
            by_square = weight * scale * scale
            by_a = weight * (2.0 * t * scale) * (1.0 - cosine)
            by_one = weight * (t2 * (1.0 - 2.0 * cosine) + t2 * cosine**2 + (t2 - 1.0) * sine_square)
            quadratics.append((by_square * square + by_a * a + by_one * identity).astype(bf16))
        factors.append(quadratics)
        errors.append(1.0 / (top * top))
    yield
    narrow = [dot(*pair).astype(bf16) for pair in factors]
    yield
    defects = [2.0 * identity - dot(p[0], x) for p, x in zip(parts, narrow)]
    yield
    seconds = [
        (2.0 / (2.0 - error)) * dot(x, e.astype(bf16))
        for x, e, error in zip(narrow, defects, errors)
    ]
    yield
    wide = [x.astype(bf16) for x in seconds]
    rests = [identity - dot_both(p, x) for p, x in zip(parts, wide)]
    yield
    small = [r.astype(bf16) for r in rests]
    sums = [r + dot(s, s) for r, s in zip(rests, small)]
    yield
    inverses = [x.astype(f32) + dot(x, s.astype(bf16)) for x, s in zip(wide, sums)]
    yield
    return inverses, ratios


def traces_of(field, gather):
    high, middle, low = thirds(field)
    stacked = jnp.concatenate([high.astype(f32), middle.astype(f32), low.astype(f32)], axis=0)
    out = dot(stacked.astype(bf16), gather)
    return out[0:8] + (out[8:16] + out[16:24])


def at_even(axis):
    return lax.rem(lax.axis_index(axis), 2) == 0


def store_traces(traces, refs):
    for d, axis in enumerate(AXES):
        even = at_even(axis)
        lower = traces[:, 2 * LANES * d : 2 * LANES * d + LANES]
        upper = traces[:, 2 * LANES * d + LANES : 2 * LANES * (d + 1)]
        refs[2 * d][...] = jnp.where(even, upper, lower)
        refs[2 * d + 1][...] = jnp.where(even, lower, upper)


def apply_inverses(inverse_ref, columns):
    rows = []
    for e in range(CELLS):
        rows.append(jnp.sum(inverse_ref[e] * columns[:, e : e + 1], axis=0, keepdims=True))
    return jnp.concatenate(rows, axis=0)


def rows_of(ref):
    return jnp.concatenate([ref[y] for y in range(ref.shape[0])], axis=0)


GROUP = 2


def staggered(groups):
    waiting, running = list(groups), []
    while waiting or running:
        if waiting:
            running.append(waiting.pop(0))
        running = [group for group in running if next(group, running) is not running]


def inverse_stages(elements, factor_ref, masses, inverse_ref, ratios):
    lows = []
    heads, crosses, tails = [], [], []
    for e in elements:
        factor = factor_ref[e]
        factor_t = factor.T
        scale = 1.0 / UNKNOWNS
        mass = masses[e : e + 1, :]
        lows.append(jnp.min(mass, axis=1, keepdims=True))
        left = scale * dot(factor_t[:HEAD], factor[:, :HEAD])
        right = scale * dot(factor_t, factor[:, HEAD:])
        heads.append(left + jnp.where(eye_mask(HEAD), mass[:, :HEAD], 0.0))
        crosses.append(right[:HEAD])
        tails.append(right[HEAD:] + jnp.where(eye_mask(TAIL), mass[:, HEAD:], 0.0))
    yield
    firsts, more = yield from approximate_inverses(heads, lows)
    ratios += more
    first_parts = [halves(x) for x in firsts]
    cross_parts = [halves(c) for c in crosses]
    carried = [dot_split(p, c) for p, c in zip(first_parts, cross_parts)]
    yield
    carried_parts = [halves(c) for c in carried]
    schurs = [
        tail - dot_split([part.T for part in cross], c)
        for tail, cross, c in zip(tails, cross_parts, carried_parts)
    ]
    yield
    lasts, more = yield from approximate_inverses(schurs, lows)
    ratios += more
    last_parts = [halves(x) for x in lasts]
    for k, e in enumerate(elements):
        corner = -dot_split(carried_parts[k], last_parts[k])
        inverse_ref[e, HEAD:, HEAD:] = lasts[k]
        inverse_ref[e, :HEAD, HEAD:] = corner
        inverse_ref[e, HEAD:, :HEAD] = corner.T
        inverse_ref[e, :HEAD, :HEAD] = firsts[k] - dot_split_nt(halves(corner), carried_parts[k])


def invert_kernel(
    factor_ref, mass_ref, flags_ref, residual_ref, gather_hbm, wall_hbm, sides_hbm,
    inverse_ref, walls_ref, opens_ref, columns_ref, field_ref, *refs
):
    trace_refs, (wall_ref, sides_ref, gather_ref, sems) = refs[:6], refs[6:]
    targets = (wall_ref, sides_ref, gather_ref)
    loads = [
        pltpu.make_async_copy(source, target, sems.at[k])
        for k, (source, target) in enumerate(zip((wall_hbm, sides_hbm, gather_hbm), targets))
    ]
    for load in loads:
        load.start()
    masses = rows_of(mass_ref)
    columns = rows_of(residual_ref).T
    columns_ref[...] = columns
    ratios = []
    groups = [
        inverse_stages(range(start, start + GROUP), factor_ref, masses, inverse_ref, ratios)
        for start in range(0, CELLS, GROUP)
    ]
    staggered(groups)
    worst = ratios[0]
    for ratio in ratios[1:]:
        worst = jnp.maximum(worst, ratio)

    @pl.when(jnp.logical_not(jnp.max(worst) <= CONDITION_LIMIT))
    def _():
        diagonal = eye_mask(UNKNOWNS)
        lane = lax.broadcasted_iota(jnp.int32, (1, UNKNOWNS), 1)
        line = lax.broadcasted_iota(jnp.int32, (UNKNOWNS, 1), 0)

        def element(e, carry):
            factor = factor_ref[e]
            line8 = lax.broadcasted_iota(jnp.int32, (CELLS, 1), 0)
            mass = jnp.sum(jnp.where(line8 == e, masses, 0.0), axis=0, keepdims=True)
            inverse_ref[e] = dot(factor.T, factor) / UNKNOWNS + jnp.where(diagonal, mass, 0.0)

            def sweep(k, inner):
                table = inverse_ref[e]
                row = inverse_ref[e, pl.ds(k, 1), :]
                column = jnp.sum(jnp.where(diagonal, row, 0.0), axis=1, keepdims=True)
                pivot = jnp.sum(jnp.where(lane == k, row, 0.0), axis=1, keepdims=True)
                scaled = row / pivot
                swept = table - column * scaled
                swept = jnp.where(line == k, scaled, swept)
                swept = jnp.where(lane == k, column / pivot, swept)
                swept = jnp.where((line == k) & (lane == k), -1.0 / pivot, swept)
                inverse_ref[e] = swept
                return inner

            lax.fori_loop(0, UNKNOWNS, sweep, 0)
            inverse_ref[e] = -inverse_ref[e]
            return carry

        lax.fori_loop(0, CELLS, element, 0)

    field = apply_inverses(inverse_ref, columns)
    field_ref[...] = field
    for load in loads:
        load.wait()
    flags = rows_of(flags_ref).astype(f32).astype(bf16)
    walls_ref[...] = wall_weight * dot(flags, wall_ref[...])
    open_sides = 1.0 - dot_nt(sides_ref[...], flags)
    side_lane = lax.broadcasted_iota(jnp.int32, (FACE, CELLS), 1)
    for d, axis in enumerate(AXES):
        step, count = STEPS[d], COUNTS[d]
        has_above = lax.axis_index(axis) < lax.axis_size(axis) - 1
        at_top = (side_lane // step) % count == count - 1
        opens_ref[2 * d * FACE : (2 * d + 1) * FACE] = -open_sides[2 * d * FACE : (2 * d + 1) * FACE]
        opens_ref[(2 * d + 1) * FACE : (2 * d + 2) * FACE] = jnp.where(
            jnp.logical_and(at_top, jnp.logical_not(has_above)),
            0.0,
            open_sides[(2 * d + 1) * FACE : (2 * d + 2) * FACE],
        )
    store_traces(traces_of(field, gather_ref[...]), trace_refs)


def widened(trace):
    return jnp.concatenate([trace, jnp.zeros_like(trace)], axis=1)


def coupled(
    field_ref, walls_ref, opens_ref, face_ref, tops, own, received, scatter_ref
):
    lane8 = lax.broadcasted_iota(jnp.int32, (FACE, CELLS), 1)
    pieces = []
    for d, axis in enumerate(AXES):
        here = lax.axis_index(axis)
        has_below = here > 0
        even = at_even(axis)
        sent, got = own[2 * d : 2 * d + 2], received[2 * d : 2 * d + 2]
        lower = jnp.where(even, sent[1][...], sent[0][...])
        lower = pltpu.roll(widened(lower), FACE, 1)
        upper = widened(jnp.where(even, sent[0][...], sent[1][...]))
        below = jnp.where(even, got[1][...], got[0][...])
        below = widened(jnp.where(has_below, below, 0.0))
        above = jnp.where(even, got[0][...], got[1][...])
        above = pltpu.roll(widened(above), FACE, 1)
        step, count = STEPS[d], COUNTS[d]
        faces = CELLS // count
        rest = above[:, LANES:]
        rests = [rest] + [pltpu.roll(rest, 32 * k, 1) for k in range(1, min(faces, 4))]
        low_part = jnp.zeros((FACE, CELLS), f32)
        high_part = jnp.zeros((FACE, CELLS), f32)
        for e in range(CELLS):
            spot = (e // step) % count
            if spot == 0:
                other = e + step * (count - 1)
                left = below[other : other + 1]
            else:
                left = upper[e - step : e - step + 1]
            pair = left + lower[e : e + 1]
            flux = jnp.sum(face_ref[e, d] * pair[:, : 2 * FACE], axis=1, keepdims=True)
            low_part = jnp.where(lane8 == e, flux, low_part)
            if spot > 0:
                high_part = jnp.where(lane8 == e - step, flux, high_part)
            if spot == count - 1:
                first = e - step * (count - 1)
                slot = (e, e - 6, e // 2)[d]
                pair = upper[e : e + 1, :LANES] + above[first : first + 1, :LANES]
                tail = rests[slot % 4][first : first + 1]
                flux = jnp.sum(
                    tops[d][slot] * pair + tops[d][faces + slot // 4] * tail, axis=1, keepdims=True
                )
                high_part = jnp.where(lane8 == e, flux, high_part)
        pieces += [low_part, high_part]
    flux_columns = opens_ref[...] * jnp.concatenate(pieces, axis=0)
    scatter = scatter_ref[...]
    high, middle, low = thirds(flux_columns)
    columns = dot(scatter, high) + (dot(scatter, middle) + dot(scatter, low))
    return columns + (walls_ref[...] * field_ref[...]).T


def split_refs(refs):
    own, received, tops = refs[:6], refs[6:12], refs[12:15]
    return own, received, tops, refs[15:]


def step_kernel(inverse_ref, walls_ref, opens_ref, gather_ref, scatter_ref, field_ref, face_ref, *refs):
    own, received, tops, outs = split_refs(refs)
    columns = coupled(field_ref, walls_ref, opens_ref, face_ref, tops, own, received, scatter_ref)
    outs[0][...] = columns
    field = apply_inverses(inverse_ref, columns)
    outs[1][...] = field
    store_traces(traces_of(field, gather_ref[...]), outs[2:])


def dots_kernel(walls_ref, opens_ref, scatter_ref, field_ref, face_ref, first_ref, second_ref, third_ref, *refs):
    own, received, tops, outs = split_refs(refs)
    last = coupled(field_ref, walls_ref, opens_ref, face_ref, tops, own, received, scatter_ref)
    vectors = [first_ref[...], second_ref[...], third_ref[...], last]
    lane = lax.broadcasted_iota(jnp.int32, (8, LANES), 1)
    packed = jnp.zeros((8, LANES), f32)
    for i in range(4):
        for j in range(i, 4):
            value = jnp.sum(jnp.sum(vectors[i] * vectors[j], axis=0, keepdims=True), axis=1, keepdims=True)
            packed = jnp.where(lane == 4 * i + j, value, packed)
    outs[0][...] = packed


def least_squares(columns, start_norm):
    count = len(columns)
    cosines = []
    sine_terms = []
    target_values = [start_norm] + [jnp.zeros_like(start_norm) for i in range(count)]
    triangle = []
    for j in range(count):
        column = list(columns[j])
        for i in range(j):
            first_entry = column[i]
            second_entry = column[i + 1]
            column[i] = cosines[i] * first_entry + sine_terms[i] * second_entry
            column[i + 1] = -sine_terms[i] * first_entry + cosines[i] * second_entry
        radius = jnp.sqrt(column[j] * column[j] + column[j + 1] * column[j + 1])
        used = radius > 0.0
        divisor = jnp.where(used, radius, 1.0)
        cosine = jnp.where(used, column[j] / divisor, 1.0)
        sine_part = jnp.where(used, column[j + 1] / divisor, 0.0)
        cosines.append(cosine)
        sine_terms.append(sine_part)
        column[j] = radius
        target_values[j + 1] = -sine_part * target_values[j]
        target_values[j] = cosine * target_values[j]
        triangle.append(column[: j + 1])
    weights = [None] * count
    for i in reversed(range(count)):
        running = target_values[i]
        for k in range(i + 1, count):
            running = running - triangle[k][i] * weights[k]
        used = triangle[i][i] > 0.0
        weights[i] = jnp.where(used, running / jnp.where(used, triangle[i][i], 1.0), 0.0)
    return weights


def finish_kernel(partial_ref, first_ref, second_ref, third_ref, out_ref):
    totals = jnp.sum(partial_ref[...], axis=0, keepdims=True)
    lane = lax.broadcasted_iota(jnp.int32, (1, LANES), 1)

    def entry(i, j):
        return jnp.sum(jnp.where(lane == 4 * i + j, totals, 0.0), axis=1, keepdims=True)

    upper = [[None] * 4 for i in range(4)]
    for i in range(4):
        for j in range(i, 4):
            square = entry(i, j)
            value = square
            for k in range(i):
                value = value - upper[k][i] * upper[k][j]
            if i == j:
                upper[i][i] = jnp.where(value > 1e-6 * square, jnp.sqrt(jnp.maximum(value, 0.0)), 0.0)
            else:
                used = upper[i][i] > 0.0
                upper[i][j] = jnp.where(used, value / jnp.where(used, upper[i][i], 1.0), 0.0)
    columns = []
    for j in range(KRYLOV):
        column = []
        for i in range(j + 2):
            value = upper[i][j + 1]
            if i <= j:
                value = value + upper[i][j]
            column.append(value)
        columns.append(column)
    weights = least_squares(columns, upper[0][0])
    update = weights[0] * first_ref[...] + weights[1] * second_ref[...] + weights[2] * third_ref[...]
    for y in range(COUNTS[1]):
        out_ref[y] = update[2 * y : 2 * y + 2]


def vmem(count):
    return [pl.BlockSpec(memory_space=pltpu.VMEM)] * count


def slabs_kernel(face_hbm, factor_hbm, mass_hbm, flags_hbm, residual_hbm, *refs):
    outs, kept, (slab_ref, sems) = refs[:3], refs[3:7], refs[7:]
    pairs = [
        (face_hbm.at[:, 0], slab_ref.at[:CELLS]),
        (face_hbm.at[:2, 1], slab_ref.at[CELLS : CELLS + 2]),
    ]
    pairs += [(face_hbm.at[2 * k, 2], slab_ref.at[CELLS + 2 + k]) for k in range(4)]
    loads = []
    for k, (source, target) in enumerate(pairs):
        loads.append(pltpu.make_async_copy(source, target, sems.at[k]))
        loads[-1].start()
    others = []
    for k, (source, target) in enumerate(zip((factor_hbm, mass_hbm, flags_hbm, residual_hbm), kept)):
        others.append(pltpu.make_async_copy(source, target, sems.at[len(pairs) + k]))
        others[-1].start()
    for load in loads:
        load.wait()
    for d, (start, count) in enumerate(((0, CELLS), (CELLS, 2), (CELLS + 2, 4))):
        out = outs[d]
        for slot in range(count):
            out[slot] = slab_ref[start + slot, :, :LANES]
        for first in range(0, count, 4):
            group = [
                slab_ref[start + slot, :, LANES:] for slot in range(first, min(first + 4, count))
            ]
            if len(group) < 4:
                group.append(jnp.zeros((FACE, LANES - 32 * len(group)), f32))
            out[count + first // 4] = jnp.concatenate(group, axis=1)
    for load in others:
        load.wait()


HBM_SPEC = pl.BlockSpec(memory_space=pltpu.HBM)


def call(kernel, specs, shapes, name, megabytes, args, scratch=()):
    args = [
        pltpu.with_memory_space_constraint(arg, pltpu.HBM) if spec is HBM_SPEC else arg
        for arg, spec in zip(args, specs)
    ]
    return pl.pallas_call(
        kernel,
        out_shape=[
            shape if isinstance(shape, jax.ShapeDtypeStruct) else jax.ShapeDtypeStruct(shape, f32)
            for shape in shapes
        ],
        in_specs=specs,
        out_specs=vmem(len(shapes)),
        scratch_shapes=scratch,
        name=name,
        compiler_params=pltpu.CompilerParams(vmem_limit_bytes=megabytes << 20),
    )(*args)


TRACE_SHAPES = [(CELLS, LANES)] * 6
INVERT_SHAPES = [
    (CELLS, UNKNOWNS, UNKNOWNS),
    (CELLS, UNKNOWNS),
    (6 * FACE, CELLS),
    (UNKNOWNS, CELLS),
    (CELLS, UNKNOWNS),
] + TRACE_SHAPES
INVERT_SCRATCH = [
    pltpu.VMEM((6, UNKNOWNS), bf16),
    pltpu.VMEM((6 * FACE, 6), bf16),
    pltpu.VMEM((UNKNOWNS, 6 * LANES), bf16),
    pltpu.SemaphoreType.DMA((3,)),
]
SLAB_SHAPES = [(10, FACE, LANES), (3, FACE, LANES), (5, FACE, LANES)]


def around(block, axis, distance):
    count = lax.axis_size(axis)
    return lax.ppermute(block, axis, [(i, (i + distance) % count) for i in range(count)])


def exchanged(own):
    received = []
    for d, axis in enumerate(AXES):
        count = lax.axis_size(axis)
        pairs = [(i, i ^ 1) for i in range(count)]
        received.append(lax.ppermute(own[2 * d], axis, pairs))
        pairs = [(i, (((i + 1) ^ 1) - 1) % count) for i in range(count)]
        received.append(lax.ppermute(own[2 * d + 1], axis, pairs))
    return received


def shards(flux_jacobian_factor, mass_over_timestep, face_jacobian, face_flags, right_side):
    gather = jnp.asarray(gather_matrix(), bf16)
    scatter = jnp.asarray(scatter_matrix(), bf16)
    wall = jnp.asarray(wall_table(), bf16)
    sides = jnp.asarray(side_table(), bf16)
    faces = face_jacobian.reshape(CELLS, 3, FACE, 2 * FACE)
    operands = (
        flux_jacobian_factor.reshape(CELLS, UNKNOWNS, UNKNOWNS),
        mass_over_timestep.reshape(4, 2, UNKNOWNS),
        face_flags.reshape(4, 2, 6),
        right_side.reshape(4, 2, UNKNOWNS),
    )
    *slabs, factor, mass, flags, residual = call(
        slabs_kernel,
        [HBM_SPEC] * 5,
        SLAB_SHAPES + [jax.ShapeDtypeStruct(a.shape, a.dtype) for a in operands],
        "slabs",
        8,
        (faces, *operands),
        [pltpu.VMEM((14, FACE, 2 * FACE), f32), pltpu.SemaphoreType.DMA((10,))],
    )
    tops = [around(slab, axis, -1) for slab, axis in zip(slabs, AXES)]
    inverse, walls, opens, columns, field, *own = call(
        invert_kernel,
        vmem(4) + [HBM_SPEC] * 3,
        INVERT_SHAPES,
        "invert",
        INVERT_MIB,
        (factor, mass, flags, residual, gather, wall, sides),
        INVERT_SCRATCH,
    )
    vectors, fields = [columns], [field]
    for j in range(KRYLOV - 1):
        received = exchanged(own)
        columns, field, *own = call(
            step_kernel,
            vmem(22),
            [(UNKNOWNS, CELLS), (CELLS, UNKNOWNS)] + TRACE_SHAPES,
            "step",
            STEP_MIB,
            (inverse, walls, opens, gather, scatter, fields[j], faces, *own, *received, *tops),
        )
        vectors.append(columns)
        fields.append(field)
    received = exchanged(own)
    (packed,) = call(
        dots_kernel,
        vmem(23),
        [(8, LANES)],
        "dots",
        STEP_MIB,
        (walls, opens, scatter, fields[2], faces, *vectors, *own, *received, *tops),
    )
    devices = lax.axis_size("gx") * lax.axis_size("gy") * lax.axis_size("gz")
    spread = jnp.broadcast_to(packed[0:1], (devices, LANES))
    partial = lax.all_to_all(spread, AXES, 0, 0, tiled=True)
    (update,) = call(
        finish_kernel, vmem(4), [(4, 2, UNKNOWNS)], "finish", 8, (partial, *fields)
    )
    return update.reshape(right_side.shape)


def solution(mesh):
    in_specs = (
        P("gx", "gy", "gz", None, None),
        P("gx", "gy", "gz", None),
        P("gx", "gy", "gz", None, None, None),
        P("gx", "gy", "gz", None),
        P("gx", "gy", "gz", None),
    )
    out_specs = P("gx", "gy", "gz", None)
    return jax.shard_map(shards, mesh=mesh, in_specs=in_specs, out_specs=out_specs, check_vma=False)
```

```python
import jax
import jax.numpy as jnp
import numpy as np
from jax import lax
from jax.experimental import pallas as pl
from jax.experimental.pallas import tpu as pltpu
from jax.sharding import PartitionSpec as P

VARS = 5
ORDER = 4
KRYLOV = 3
UNKNOWNS = 320
FACE = 80
HEAD = 128
TAIL = UNKNOWNS - HEAD
CELLS = 8
LANES = 128
CONDITION_LIMIT = 26.0
wall_weight = 0.5
INVERT_MIB = 28
STEP_MIB = 16


f32 = jnp.float32
bf16 = jnp.bfloat16
AXES = ("gx", "gy", "gz")
COUNTS = (1, 4, 2)
STEPS = (CELLS, 2, 1)


def face_nodes():
    cube = np.arange(UNKNOWNS).reshape(VARS, ORDER, ORDER, ORDER)
    nodes = []
    for d in range(3):
        for index in (0, ORDER - 1):
            nodes.append(np.take(cube, index, axis=1 + d).reshape(-1))
    return nodes


def gather_matrix():
    table = np.zeros((UNKNOWNS, 6 * LANES), np.float32)
    for side, nodes in enumerate(face_nodes()):
        for k in range(FACE):
            table[nodes[k], LANES * side + k] = 1.0
    return table


def scatter_matrix():
    table = np.zeros((UNKNOWNS, 6 * FACE), np.float32)
    for side, nodes in enumerate(face_nodes()):
        for k in range(FACE):
            table[nodes[k], FACE * side + k] = 1.0
    return table


def side_table():
    return np.repeat(np.eye(6, dtype=np.float32), FACE, axis=0)


def wall_table():
    table = np.zeros((6, UNKNOWNS), np.float32)
    for side, nodes in enumerate(face_nodes()):
        table[side, nodes] = 1.0
    return table


def dot(a, b):
    return jnp.dot(a, b, preferred_element_type=f32)


def dot_nt(a, b):
    return lax.dot_general(a, b, (((1,), (1,)), ((), ())), preferred_element_type=f32)


def halves(a):
    high = a.astype(bf16)
    return high, (a - high.astype(f32)).astype(bf16)


def thirds(a):
    high = a.astype(bf16)
    rest = a - high.astype(f32)
    middle = rest.astype(bf16)
    return high, middle, (rest - middle.astype(f32)).astype(bf16)


def dot_both(a, b):
    rows = a[0].shape[0]
    both = dot(jnp.concatenate(a, axis=0), b)
    return both[:rows] + both[rows:]


def dot_split(a, b):
    return dot_both(a, b[0]) + dot(a[0], b[1])


def dot_split_nt(a, b):
    rows = a[0].shape[0]
    both = dot_nt(jnp.concatenate(a, axis=0), b[0])
    return both[:rows] + (both[rows:] + dot_nt(a[0], b[1]))


def eye_mask(n):
    rows = lax.broadcasted_iota(jnp.int32, (n, n), 0)
    cols = lax.broadcasted_iota(jnp.int32, (n, n), 1)
    return rows == cols


def approximate_inverses(blocks, lows):
    n = blocks[0].shape[0]
    diagonal = eye_mask(n)
    identity = jnp.where(diagonal, 1.0, 0.0)
    parts = [halves(a) for a in blocks]
    squares = [dot(p[0], p[0]) for p in parts]
    firsts, errors, ratios = [], [], []
    for a, square, low in zip(blocks, squares, lows):
        sums = jnp.sum(jnp.abs(square), axis=0, keepdims=True)
        high = 1.03 * jnp.sqrt(jnp.max(sums, axis=1, keepdims=True))
        high = jnp.maximum(high, 1.1 * low)
        ratios.append(high / low)
        half = 0.5 * (high - low)
        scale = 1.0 / half
        t = -0.5 * (high + low) * scale
        t2 = t * t
        c3 = 16.0 * t
        c2 = 16.0 * t2 - 20.0
        c1 = t * c2
        c0 = t2 * c2 + 5.0
        top = t * c0
        gain = -scale / top
        square_scale = scale * scale
        slope = 2.0 * t * scale
        inner_slope = c3 * scale + 16.0 * slope
        both = c3 * t + 16.0 * t2
        outer = square_scale * square + slope * a
        inner = (16.0 * gain * square_scale) * square + (gain * inner_slope) * a
        by_square = gain * square_scale * (16.0 * t2 + both + c2)
        by_a = gain * (t2 * inner_slope + both * slope + c1 * scale + c2 * slope)
        by_one = gain * (t2 * both + c1 * t + c2 * t2 + c0)
        base = by_square * square + by_a * a + by_one * identity
        firsts.append(base + dot(outer.astype(bf16), inner.astype(bf16)))
        errors.append(1.0 / (top * top))
    narrow = [x.astype(bf16) for x in firsts]
    defects = [2.0 * identity - dot(p[0], x) for p, x in zip(parts, narrow)]
    seconds = [
        (2.0 / (2.0 - error)) * dot(x, e.astype(bf16))
        for x, e, error in zip(narrow, defects, errors)
    ]
    wide = [x.astype(bf16) for x in seconds]
    rests = [identity - dot_both(p, x) for p, x in zip(parts, wide)]
    small = [r.astype(bf16) for r in rests]
    sums = [r + dot(s, s) for r, s in zip(rests, small)]
    inverses = [x.astype(f32) + dot(x, s.astype(bf16)) for x, s in zip(wide, sums)]
    return inverses, ratios


def traces_of(field, gather):
    high, middle, low = thirds(field)
    stacked = jnp.concatenate([high.astype(f32), middle.astype(f32), low.astype(f32)], axis=0)
    out = dot(stacked.astype(bf16), gather)
    return out[0:8] + (out[8:16] + out[16:24])


def at_even(axis):
    return lax.rem(lax.axis_index(axis), 2) == 0


def store_traces(traces, refs):
    for d, axis in enumerate(AXES):
        even = at_even(axis)
        lower = traces[:, 2 * LANES * d : 2 * LANES * d + LANES]
        upper = traces[:, 2 * LANES * d + LANES : 2 * LANES * (d + 1)]
        refs[2 * d][...] = jnp.where(even, upper, lower)
        refs[2 * d + 1][...] = jnp.where(even, lower, upper)


def apply_inverses(inverse_ref, columns):
    rows = []
    for e in range(CELLS):
        rows.append(jnp.sum(inverse_ref[e] * columns[:, e : e + 1], axis=0, keepdims=True))
    return jnp.concatenate(rows, axis=0)


def rows_of(ref):
    return jnp.concatenate([ref[y] for y in range(ref.shape[0])], axis=0)


def invert_kernel(
    factor_ref, mass_ref, flags_ref, residual_ref, gather_hbm, wall_hbm, sides_hbm,
    inverse_ref, walls_ref, opens_ref, columns_ref, field_ref, *refs
):
    trace_refs, (wall_ref, sides_ref, gather_ref, sems) = refs[:6], refs[6:]
    targets = (wall_ref, sides_ref, gather_ref)
    loads = [
        pltpu.make_async_copy(source, target, sems.at[k])
        for k, (source, target) in enumerate(zip((wall_hbm, sides_hbm, gather_hbm), targets))
    ]
    for load in loads:
        load.start()
    masses = rows_of(mass_ref)
    columns = rows_of(residual_ref).T
    columns_ref[...] = columns
    lows = []
    heads, crosses, backs, tails = [], [], [], []
    for e in range(CELLS):
        factor = factor_ref[e]
        factor_t = factor.T
        scale = 1.0 / UNKNOWNS
        mass = masses[e : e + 1, :]
        lows.append(jnp.min(mass, axis=1, keepdims=True))
        left = scale * dot(factor_t, factor[:, :HEAD])
        right = scale * dot(factor_t, factor[:, HEAD:])
        heads.append(left[:HEAD] + jnp.where(eye_mask(HEAD), mass[:, :HEAD], 0.0))
        backs.append(left[HEAD:])
        crosses.append(right[:HEAD])
        tails.append(right[HEAD:] + jnp.where(eye_mask(TAIL), mass[:, HEAD:], 0.0))
    firsts, ratios = approximate_inverses(heads, lows)
    first_parts = [halves(x) for x in firsts]
    carried = [dot_split(p, halves(c)) for p, c in zip(first_parts, crosses)]
    carried_parts = [halves(c) for c in carried]
    schurs = [
        tail - dot_split(halves(back), c) for tail, back, c in zip(tails, backs, carried_parts)
    ]
    lasts, more = approximate_inverses(schurs, lows)
    last_parts = [halves(x) for x in lasts]
    for e in range(CELLS):
        corner = -dot_split(carried_parts[e], last_parts[e])
        inverse_ref[e, HEAD:, HEAD:] = lasts[e]
        inverse_ref[e, :HEAD, HEAD:] = corner
        inverse_ref[e, HEAD:, :HEAD] = corner.T
        inverse_ref[e, :HEAD, :HEAD] = firsts[e] - dot_split_nt(halves(corner), carried_parts[e])
    worst = ratios[0]
    for ratio in ratios[1:] + more:
        worst = jnp.maximum(worst, ratio)

    @pl.when(jnp.logical_not(jnp.max(worst) <= CONDITION_LIMIT))
    def _():
        diagonal = eye_mask(UNKNOWNS)
        lane = lax.broadcasted_iota(jnp.int32, (1, UNKNOWNS), 1)
        line = lax.broadcasted_iota(jnp.int32, (UNKNOWNS, 1), 0)

        def element(e, carry):
            factor = factor_ref[e]
            line8 = lax.broadcasted_iota(jnp.int32, (CELLS, 1), 0)
            mass = jnp.sum(jnp.where(line8 == e, masses, 0.0), axis=0, keepdims=True)
            inverse_ref[e] = dot(factor.T, factor) / UNKNOWNS + jnp.where(diagonal, mass, 0.0)

            def sweep(k, inner):
                table = inverse_ref[e]
                row = inverse_ref[e, pl.ds(k, 1), :]
                column = jnp.sum(jnp.where(diagonal, row, 0.0), axis=1, keepdims=True)
                pivot = jnp.sum(jnp.where(lane == k, row, 0.0), axis=1, keepdims=True)
                scaled = row / pivot
                swept = table - column * scaled
                swept = jnp.where(line == k, scaled, swept)
                swept = jnp.where(lane == k, column / pivot, swept)
                swept = jnp.where((line == k) & (lane == k), -1.0 / pivot, swept)
                inverse_ref[e] = swept
                return inner

            lax.fori_loop(0, UNKNOWNS, sweep, 0)
            inverse_ref[e] = -inverse_ref[e]
            return carry

        lax.fori_loop(0, CELLS, element, 0)

    field = apply_inverses(inverse_ref, columns)
    field_ref[...] = field
    for load in loads:
        load.wait()
    flags = rows_of(flags_ref).astype(f32).astype(bf16)
    walls_ref[...] = wall_weight * dot(flags, wall_ref[...])
    open_sides = 1.0 - dot_nt(sides_ref[...], flags)
    side_lane = lax.broadcasted_iota(jnp.int32, (FACE, CELLS), 1)
    for d, axis in enumerate(AXES):
        step, count = STEPS[d], COUNTS[d]
        has_above = lax.axis_index(axis) < lax.axis_size(axis) - 1
        at_top = (side_lane // step) % count == count - 1
        opens_ref[2 * d * FACE : (2 * d + 1) * FACE] = -open_sides[2 * d * FACE : (2 * d + 1) * FACE]
        opens_ref[(2 * d + 1) * FACE : (2 * d + 2) * FACE] = jnp.where(
            jnp.logical_and(at_top, jnp.logical_not(has_above)),
            0.0,
            open_sides[(2 * d + 1) * FACE : (2 * d + 2) * FACE],
        )
    store_traces(traces_of(field, gather_ref[...]), trace_refs)


def widened(trace):
    return jnp.concatenate([trace, jnp.zeros_like(trace)], axis=1)


def coupled(
    field_ref, walls_ref, opens_ref, face_ref, tops, own, received, scatter_ref
):
    lane8 = lax.broadcasted_iota(jnp.int32, (FACE, CELLS), 1)
    pieces = []
    for d, axis in enumerate(AXES):
        here = lax.axis_index(axis)
        has_below = here > 0
        even = at_even(axis)
        sent, got = own[2 * d : 2 * d + 2], received[2 * d : 2 * d + 2]
        lower = jnp.where(even, sent[1][...], sent[0][...])
        lower = pltpu.roll(widened(lower), FACE, 1)
        upper = widened(jnp.where(even, sent[0][...], sent[1][...]))
        below = jnp.where(even, got[1][...], got[0][...])
        below = widened(jnp.where(has_below, below, 0.0))
        above = jnp.where(even, got[0][...], got[1][...])
        above = pltpu.roll(widened(above), FACE, 1)
        step, count = STEPS[d], COUNTS[d]
        faces = CELLS // count
        rest = above[:, LANES:]
        rests = [rest] + [pltpu.roll(rest, 32 * k, 1) for k in range(1, min(faces, 4))]
        low_part = jnp.zeros((FACE, CELLS), f32)
        high_part = jnp.zeros((FACE, CELLS), f32)
        for e in range(CELLS):
            spot = (e // step) % count
            if spot == 0:
                other = e + step * (count - 1)
                left = below[other : other + 1]
            else:
                left = upper[e - step : e - step + 1]
            pair = left + lower[e : e + 1]
            flux = jnp.sum(face_ref[e, d] * pair[:, : 2 * FACE], axis=1, keepdims=True)
            low_part = jnp.where(lane8 == e, flux, low_part)
            if spot > 0:
                high_part = jnp.where(lane8 == e - step, flux, high_part)
            if spot == count - 1:
                first = e - step * (count - 1)
                slot = (e, e - 6, e // 2)[d]
                pair = upper[e : e + 1, :LANES] + above[first : first + 1, :LANES]
                tail = rests[slot % 4][first : first + 1]
                flux = jnp.sum(
                    tops[d][slot] * pair + tops[d][faces + slot // 4] * tail, axis=1, keepdims=True
                )
                high_part = jnp.where(lane8 == e, flux, high_part)
        pieces += [low_part, high_part]
    flux_columns = opens_ref[...] * jnp.concatenate(pieces, axis=0)
    scatter = scatter_ref[...]
    high, low = halves(flux_columns)
    columns = dot(scatter, high) + dot(scatter, low)
    return columns + (walls_ref[...] * field_ref[...]).T


def split_refs(refs):
    own, received, tops = refs[:6], refs[6:12], refs[12:15]
    return own, received, tops, refs[15:]


def step_kernel(inverse_ref, walls_ref, opens_ref, gather_ref, scatter_ref, field_ref, face_ref, *refs):
    own, received, tops, outs = split_refs(refs)
    columns = coupled(field_ref, walls_ref, opens_ref, face_ref, tops, own, received, scatter_ref)
    outs[0][...] = columns
    field = apply_inverses(inverse_ref, columns)
    outs[1][...] = field
    store_traces(traces_of(field, gather_ref[...]), outs[2:])


def dots_kernel(walls_ref, opens_ref, scatter_ref, field_ref, face_ref, first_ref, second_ref, third_ref, *refs):
    own, received, tops, outs = split_refs(refs)
    last = coupled(field_ref, walls_ref, opens_ref, face_ref, tops, own, received, scatter_ref)
    vectors = [first_ref[...], second_ref[...], third_ref[...], last]
    lane = lax.broadcasted_iota(jnp.int32, (8, LANES), 1)
    packed = jnp.zeros((8, LANES), f32)
    for i in range(4):
        for j in range(i, 4):
            value = jnp.sum(jnp.sum(vectors[i] * vectors[j], axis=0, keepdims=True), axis=1, keepdims=True)
            packed = jnp.where(lane == 4 * i + j, value, packed)
    outs[0][...] = packed


def least_squares(columns, start_norm):
    count = len(columns)
    cosines = []
    sine_terms = []
    target_values = [start_norm] + [jnp.zeros_like(start_norm) for i in range(count)]
    triangle = []
    for j in range(count):
        column = list(columns[j])
        for i in range(j):
            first_entry = column[i]
            second_entry = column[i + 1]
            column[i] = cosines[i] * first_entry + sine_terms[i] * second_entry
            column[i + 1] = -sine_terms[i] * first_entry + cosines[i] * second_entry
        radius = jnp.sqrt(column[j] * column[j] + column[j + 1] * column[j + 1])
        used = radius > 0.0
        divisor = jnp.where(used, radius, 1.0)
        cosine = jnp.where(used, column[j] / divisor, 1.0)
        sine_part = jnp.where(used, column[j + 1] / divisor, 0.0)
        cosines.append(cosine)
        sine_terms.append(sine_part)
        column[j] = radius
        target_values[j + 1] = -sine_part * target_values[j]
        target_values[j] = cosine * target_values[j]
        triangle.append(column[: j + 1])
    weights = [None] * count
    for i in reversed(range(count)):
        running = target_values[i]
        for k in range(i + 1, count):
            running = running - triangle[k][i] * weights[k]
        used = triangle[i][i] > 0.0
        weights[i] = jnp.where(used, running / jnp.where(used, triangle[i][i], 1.0), 0.0)
    return weights


def finish_kernel(partial_ref, first_ref, second_ref, third_ref, out_ref):
    totals = jnp.sum(partial_ref[...], axis=0, keepdims=True)
    lane = lax.broadcasted_iota(jnp.int32, (1, LANES), 1)

    def entry(i, j):
        return jnp.sum(jnp.where(lane == 4 * i + j, totals, 0.0), axis=1, keepdims=True)

    upper = [[None] * 4 for i in range(4)]
    for i in range(4):
        for j in range(i, 4):
            square = entry(i, j)
            value = square
            for k in range(i):
                value = value - upper[k][i] * upper[k][j]
            if i == j:
                upper[i][i] = jnp.where(value > 1e-6 * square, jnp.sqrt(jnp.maximum(value, 0.0)), 0.0)
            else:
                used = upper[i][i] > 0.0
                upper[i][j] = jnp.where(used, value / jnp.where(used, upper[i][i], 1.0), 0.0)
    columns = []
    for j in range(KRYLOV):
        column = []
        for i in range(j + 2):
            value = upper[i][j + 1]
            if i <= j:
                value = value + upper[i][j]
            column.append(value)
        columns.append(column)
    weights = least_squares(columns, upper[0][0])
    update = weights[0] * first_ref[...] + weights[1] * second_ref[...] + weights[2] * third_ref[...]
    for y in range(COUNTS[1]):
        out_ref[y] = update[2 * y : 2 * y + 2]


def vmem(count):
    return [pl.BlockSpec(memory_space=pltpu.VMEM)] * count


def slabs_kernel(face_hbm, factor_hbm, mass_hbm, flags_hbm, residual_hbm, *refs):
    outs, kept, (slab_ref, sems) = refs[:3], refs[3:7], refs[7:]
    pairs = [
        (face_hbm.at[:, 0], slab_ref.at[:CELLS]),
        (face_hbm.at[:2, 1], slab_ref.at[CELLS : CELLS + 2]),
    ]
    pairs += [(face_hbm.at[2 * k, 2], slab_ref.at[CELLS + 2 + k]) for k in range(4)]
    loads = []
    for k, (source, target) in enumerate(pairs):
        loads.append(pltpu.make_async_copy(source, target, sems.at[k]))
        loads[-1].start()
    others = []
    for k, (source, target) in enumerate(zip((factor_hbm, mass_hbm, flags_hbm, residual_hbm), kept)):
        others.append(pltpu.make_async_copy(source, target, sems.at[len(pairs) + k]))
        others[-1].start()
    for load in loads:
        load.wait()
    for d, (start, count) in enumerate(((0, CELLS), (CELLS, 2), (CELLS + 2, 4))):
        out = outs[d]
        for slot in range(count):
            out[slot] = slab_ref[start + slot, :, :LANES]
        for first in range(0, count, 4):
            group = [
                slab_ref[start + slot, :, LANES:] for slot in range(first, min(first + 4, count))
            ]
            if len(group) < 4:
                group.append(jnp.zeros((FACE, LANES - 32 * len(group)), f32))
            out[count + first // 4] = jnp.concatenate(group, axis=1)
    for load in others:
        load.wait()


HBM_SPEC = pl.BlockSpec(memory_space=pltpu.HBM)


def call(kernel, specs, shapes, name, megabytes, args, scratch=()):
    args = [
        pltpu.with_memory_space_constraint(arg, pltpu.HBM) if spec is HBM_SPEC else arg
        for arg, spec in zip(args, specs)
    ]
    return pl.pallas_call(
        kernel,
        out_shape=[
            shape if isinstance(shape, jax.ShapeDtypeStruct) else jax.ShapeDtypeStruct(shape, f32)
            for shape in shapes
        ],
        in_specs=specs,
        out_specs=vmem(len(shapes)),
        scratch_shapes=scratch,
        name=name,
        compiler_params=pltpu.CompilerParams(vmem_limit_bytes=megabytes << 20),
    )(*args)


TRACE_SHAPES = [(CELLS, LANES)] * 6
INVERT_SHAPES = [
    (CELLS, UNKNOWNS, UNKNOWNS),
    (CELLS, UNKNOWNS),
    (6 * FACE, CELLS),
    (UNKNOWNS, CELLS),
    (CELLS, UNKNOWNS),
] + TRACE_SHAPES
INVERT_SCRATCH = [
    pltpu.VMEM((6, UNKNOWNS), bf16),
    pltpu.VMEM((6 * FACE, 6), bf16),
    pltpu.VMEM((UNKNOWNS, 6 * LANES), bf16),
    pltpu.SemaphoreType.DMA((3,)),
]
SLAB_SHAPES = [(10, FACE, LANES), (3, FACE, LANES), (5, FACE, LANES)]


def around(block, axis, distance):
    count = lax.axis_size(axis)
    return lax.ppermute(block, axis, [(i, (i + distance) % count) for i in range(count)])


def exchanged(own):
    received = []
    for d, axis in enumerate(AXES):
        count = lax.axis_size(axis)
        pairs = [(i, i ^ 1) for i in range(count)]
        received.append(lax.ppermute(own[2 * d], axis, pairs))
        pairs = [(i, (((i + 1) ^ 1) - 1) % count) for i in range(count)]
        received.append(lax.ppermute(own[2 * d + 1], axis, pairs))
    return received


def shards(flux_jacobian_factor, mass_over_timestep, face_jacobian, face_flags, right_side):
    gather = jnp.asarray(gather_matrix(), bf16)
    scatter = jnp.asarray(scatter_matrix(), bf16)
    wall = jnp.asarray(wall_table(), bf16)
    sides = jnp.asarray(side_table(), bf16)
    faces = face_jacobian.reshape(CELLS, 3, FACE, 2 * FACE)
    operands = (
        flux_jacobian_factor.reshape(CELLS, UNKNOWNS, UNKNOWNS),
        mass_over_timestep.reshape(4, 2, UNKNOWNS),
        face_flags.reshape(4, 2, 6),
        right_side.reshape(4, 2, UNKNOWNS),
    )
    *slabs, factor, mass, flags, residual = call(
        slabs_kernel,
        [HBM_SPEC] * 5,
        SLAB_SHAPES + [jax.ShapeDtypeStruct(a.shape, a.dtype) for a in operands],
        "slabs",
        8,
        (faces, *operands),
        [pltpu.VMEM((14, FACE, 2 * FACE), f32), pltpu.SemaphoreType.DMA((10,))],
    )
    tops = [around(slab, axis, -1) for slab, axis in zip(slabs, AXES)]
    inverse, walls, opens, columns, field, *own = call(
        invert_kernel,
        vmem(4) + [HBM_SPEC] * 3,
        INVERT_SHAPES,
        "invert",
        INVERT_MIB,
        (factor, mass, flags, residual, gather, wall, sides),
        INVERT_SCRATCH,
    )
    vectors, fields = [columns], [field]
    for j in range(KRYLOV - 1):
        received = exchanged(own)
        columns, field, *own = call(
            step_kernel,
            vmem(22),
            [(UNKNOWNS, CELLS), (CELLS, UNKNOWNS)] + TRACE_SHAPES,
            "step",
            STEP_MIB,
            (inverse, walls, opens, gather, scatter, fields[j], faces, *own, *received, *tops),
        )
        vectors.append(columns)
        fields.append(field)
    received = exchanged(own)
    (packed,) = call(
        dots_kernel,
        vmem(23),
        [(8, LANES)],
        "dots",
        STEP_MIB,
        (walls, opens, scatter, fields[2], faces, *vectors, *own, *received, *tops),
    )
    devices = lax.axis_size("gx") * lax.axis_size("gy") * lax.axis_size("gz")
    spread = jnp.broadcast_to(packed[0:1], (devices, LANES))
    partial = lax.all_to_all(spread, AXES, 0, 0, tiled=True)
    (update,) = call(
        finish_kernel, vmem(4), [(4, 2, UNKNOWNS)], "finish", 8, (partial, *fields)
    )
    return update.reshape(right_side.shape)


def solution(mesh):
    in_specs = (
        P("gx", "gy", "gz", None, None),
        P("gx", "gy", "gz", None),
        P("gx", "gy", "gz", None, None, None),
        P("gx", "gy", "gz", None),
        P("gx", "gy", "gz", None),
    )
    out_specs = P("gx", "gy", "gz", None)
    return jax.shard_map(shards, mesh=mesh, in_specs=in_specs, out_specs=out_specs, check_vma=False)
```
